128 devices in a mesh: seq: 8 (over x, core), pipe: 16 (over y, z).
Axes of the slice: x: 4, y: 4, z: 4, core: 2. Of those that a mesh axis runs over, the one named last changes fastest.
Arguments:
- queries: bfloat16 [16, 1024, 8192], P('pipe', 'seq'), may hold values from -160 to 160
- layer_key_rows: bfloat16 [16, 1024, 1024], P('pipe', 'seq'), may hold values from -4 to 4
- layer_value_rows: bfloat16 [16, 1024, 1024], P('pipe', 'seq'), may hold values from -5 to 5
- vertical_blocks: int32 [16, 64, 4], P('pipe'), may hold values from 0 to 15, as said below
- slash_offsets: int32 [16, 64, 4], P('pipe'), may hold values from 0 to 15, as said below
- prompt_lengths: int32 [4], replicated, may hold values from 1 to 512, 1024 in all
- residual: bfloat16 [1024, 8192], P('seq'), may hold values from -3 to 3
- out_weight: bfloat16 [16, 8192, 8192], P('pipe', 'seq'), may hold values from -0.5 to 0.5
- section_gain: float32 [16, 8192], P('pipe'), may hold values from 0.25 to 1.75
Outputs:
- normed_hidden: bfloat16 [16, 1024, 8192], P('pipe', 'seq')
The draws below stay inside these ranges and needn't reach their ends.
Inputs may be any that keep to these rules, and one draw needn't show every extreme that they name: `vertical_blocks`: for each section and head the 4 entries are different and the first is block 0. `slash_offsets`: for each section and head the 4 entries are different and the first is offset 0. `prompt_lengths`: the lengths sum to 1024.
All inputs are finite; a program needn't handle non-finite values.
Results may differ from the reference program's by a relative error of at most 0.02.
Values may be sent and summed in bfloat16 or wider, within the bound.
No kernel may reach another device: no remote copies, remote signals or barrier semaphores. Data moves between devices by JAX's collectives and lax.ppermute only.
A program may use at most 192 MiB of HBM per device.

```python
import math
import jax
import jax.numpy as jnp
import numpy as np
from jax import lax

D = 8192
QUERY_HEADS = 64
KEY_VALUE_HEADS = 8
HEAD_SIZE = 128
BLOCK = 64
NV = 4
NS = 4
NPROMPT = 4
SPAN_TOKENS = 1024
SPAN_BLOCKS = 16
SECTION_LAYERS = 16
N_SEQ = 8


def key_lookup_table(key):
    base_offset = jax.random.truncated_normal(jax.random.fold_in(key, 17), -4.0, 4.0, (SECTION_LAYERS, SPAN_TOKENS, KEY_VALUE_HEADS * HEAD_SIZE), jnp.float32)
    return base_offset


def draw_layer_key_rows(key, part):
    return key_lookup_table(key).astype(jnp.bfloat16)


def draw_queries(key, part):
    noise = jax.random.truncated_normal(jax.random.fold_in(key, 23), -4.0, 4.0, (SECTION_LAYERS, SPAN_TOKENS, QUERY_HEADS * HEAD_SIZE), jnp.float32)
    return noise.astype(jnp.bfloat16)


def distinct_blocks(key, salt, width):
    raw = jax.random.randint(jax.random.fold_in(key, salt), (SECTION_LAYERS, QUERY_HEADS, SPAN_BLOCKS - 1), 0, 1 << 20)
    ranks = raw * SPAN_BLOCKS + jnp.arange(SPAN_BLOCKS - 1, dtype=jnp.int32)[None, None, :]
    order = jnp.argsort(ranks, axis=-1, stable=True)[..., :width - 1] + 1
    leading = jnp.zeros((SECTION_LAYERS, QUERY_HEADS, 1), jnp.int32)
    return jnp.concatenate([leading, order.astype(jnp.int32)], axis=-1)


def draw_vertical_blocks(key, part):
    return distinct_blocks(key, 41, NV)


def draw_slash_offsets(key, part):
    return distinct_blocks(key, 43, NS)


def block_levels(rng, dims, pieces, low, top_value):
    loudness, own = 1.0, jax.random.fold_in(rng, 6)
    for dim, parts in pieces:
        steps = jnp.exp(jax.random.uniform(jax.random.fold_in(own, dim), (parts,), jnp.float32, low / len(pieces), top_value / len(pieces)))
        loudness = loudness * jnp.repeat(steps, dims[dim] // parts).reshape([-1 if axis == dim else 1 for axis in range(len(dims))])
    return loudness


def split_up(count, total, reach, slope):
    portions = [(1 << 20) // math.isqrt(standing ** slope) + 1 for standing in range(2, count + 1)]
    spare, holding = total - reach - (count - 1), [1] * (count - 1)
    while spare > 0:
        free = [i for i in range(count - 1) if holding[i] < reach]
        whole, budget = sum([portions[i] for i in free]), spare
        for i in free:
            more = min(reach - holding[i], max(1, budget * portions[i] // whole), spare)
            holding[i] = holding[i] + more
            spare = spare - more
    return np.array([reach] + holding)


def ragged_sizes(stream_key, count, total, bound, skew):
    if count == 2:
        one = jax.random.randint(stream_key, (), max(1, total - bound), min(bound, total - 1) + 1)
        return jnp.stack([one, total - one])
    lengths = jnp.asarray(split_up(count, total, bound, skew), jnp.int32)
    pairs = (count - 1) // 2
    source_of, taker = lengths[1:1 + 2 * pairs:2], lengths[2:2 + 2 * pairs:2]
    margin = jnp.minimum(source_of - 1, bound - taker)
    passed = jax.random.randint(jax.random.fold_in(stream_key, 1), (pairs,), 0, 1 << 20) % (margin + 1)
    lengths = lengths.at[1:1 + 2 * pairs:2].set(source_of - passed).at[2:2 + 2 * pairs:2].set(taker + passed)
    return lengths[jax.random.permutation(jax.random.fold_in(stream_key, 2), count)]


def normal_values(own_key, shape, scale, most, pieces=(), kind=jnp.bfloat16):
    drawn = scale * jax.random.normal(own_key, shape, jnp.float32)
    if pieces:
        drawn = drawn * block_levels(own_key, shape, pieces, -0.22, 0.18)
    return jnp.clip(drawn, -most, most).astype(kind)


def setup_inputs(seed: int = 0) -> dict:
    keys = jax.random.split(jax.random.key(seed), 10)
    queries = draw_queries(jax.random.fold_in(keys[9], 71), 0)
    layer_key_rows = draw_layer_key_rows(jax.random.fold_in(keys[9], 71), 0)
    layer_value_rows = normal_values(keys[2], (SECTION_LAYERS, SPAN_TOKENS, KEY_VALUE_HEADS * HEAD_SIZE), 1.0, 5.0, ((0, 16), (1, 8)))
    vertical_blocks = draw_vertical_blocks(jax.random.fold_in(keys[9], 71), 0)
    slash_offsets = draw_slash_offsets(jax.random.fold_in(keys[9], 71), 0)
    prompt_lengths = ragged_sizes(keys[5], NPROMPT, SPAN_TOKENS, SPAN_TOKENS // 2, 2).astype(jnp.int32)
    residual = normal_values(keys[6], (SPAN_TOKENS, D), 0.5, 3.0, ((0, 8),))
    out_weight = normal_values(keys[7], (SECTION_LAYERS, QUERY_HEADS * HEAD_SIZE, D), HEAD_SIZE ** -0.5, 0.5, ((0, 16), (1, 8)))
    section_gain = jnp.clip(1.0 + 0.15 * jax.random.normal(keys[8], (SECTION_LAYERS, D), jnp.float32), 0.25, 1.75)
    return {"queries": queries, "layer_key_rows": layer_key_rows, "layer_value_rows": layer_value_rows, "vertical_blocks": vertical_blocks, "slash_offsets": slash_offsets, "prompt_lengths": prompt_lengths, "residual": residual, "out_weight": out_weight, "section_gain": section_gain}


def prompt_ids(prompt_lengths):
    starts = jnp.cumsum(prompt_lengths) - prompt_lengths
    positions = jnp.arange(SPAN_TOKENS, dtype=jnp.int32)
    return lax.optimization_barrier(jnp.sum((positions[:, None] >= starts[None, 1:]).astype(jnp.int32), axis=1))

def block_permitted(vertical_pattern, slash_pattern):
    blocks = jnp.arange(SPAN_BLOCKS, dtype=jnp.int32)
    offsets = blocks[:, None] - blocks[None, :]
    vert_hit = jnp.any(vertical_pattern[:, :, None] == blocks[None, None, :], axis=1)
    slash_hit = jnp.any(slash_pattern[:, :, None, None] == offsets[None, None, :, :], axis=1)
    return (vert_hit[:, None, :] | slash_hit) & (offsets >= 0)[None, :, :]

def section_layer(inputs, doc_ids):
    queries, layer_key_rows, layer_value_rows, vertical_pattern, slash_pattern, out_weight = inputs
    group_index = QUERY_HEADS // KEY_VALUE_HEADS
    positions = jnp.arange(SPAN_TOKENS, dtype=jnp.int32)
    tok_block = positions // BLOCK
    token_ok = (positions[None, :] <= positions[:, None]) & (doc_ids[:, None] == doc_ids[None, :])
    block_mask_table = block_permitted(vertical_pattern, slash_pattern).reshape(KEY_VALUE_HEADS, group_index, SPAN_BLOCKS, SPAN_BLOCKS)
    query_head_rows = queries.reshape(SPAN_TOKENS, KEY_VALUE_HEADS, group_index, HEAD_SIZE).transpose(1, 0, 2, 3)
    key_head_rows = layer_key_rows.reshape(SPAN_TOKENS, KEY_VALUE_HEADS, HEAD_SIZE).transpose(1, 0, 2)
    value_head_rows = layer_value_rows.reshape(SPAN_TOKENS, KEY_VALUE_HEADS, HEAD_SIZE).transpose(1, 0, 2)

    def one_group(items):
        query_group, key_group, value_group, mask_group = items
        scores = jnp.einsum('sgd,td->gst', query_group.astype(jnp.float32), key_group.astype(jnp.float32)) * (1.0 / math.sqrt(HEAD_SIZE))
        allowed = mask_group[:, tok_block][:, :, tok_block] & token_ok[None]
        masked = jnp.where(allowed, scores, -1e+30)
        largest = lax.optimization_barrier(jnp.max(masked, axis=-1, keepdims=True))
        exponent = jnp.where(allowed, jnp.exp(masked - largest), 0.0)
        weights = (exponent / lax.optimization_barrier(jnp.sum(exponent, axis=-1, keepdims=True))).astype(jnp.bfloat16)
        return jnp.einsum('gst,td->sgd', weights.astype(jnp.float32), value_group.astype(jnp.float32)).astype(jnp.bfloat16)
    context = lax.map(one_group, (query_head_rows, key_head_rows, value_head_rows, block_mask_table))
    context = context.transpose(1, 0, 2, 3)
    per_group = QUERY_HEADS // N_SEQ
    context = context.reshape(SPAN_TOKENS, N_SEQ, per_group * HEAD_SIZE).astype(jnp.float32)
    weight_groups = out_weight.reshape(N_SEQ, per_group * HEAD_SIZE, D).astype(jnp.float32)
    group_sums = jnp.einsum('sgk,gkd->gsd', context, weight_groups).astype(jnp.bfloat16)
    return lax.optimization_barrier(jnp.sum(group_sums.astype(jnp.float32), axis=0))

def reference(queries, layer_key_rows, layer_value_rows, vertical_blocks, slash_offsets, prompt_lengths, residual, out_weight, section_gain):
    doc_ids = prompt_ids(prompt_lengths)
    section_terms = lax.map(lambda inputs: section_layer(inputs, doc_ids), (queries, layer_key_rows, layer_value_rows, vertical_blocks, slash_offsets, out_weight))
    stream = residual.astype(jnp.float32)[None] + jnp.cumsum(section_terms, axis=0)
    inverse_rms = lax.rsqrt(lax.optimization_barrier(jnp.mean(stream * stream, axis=-1, keepdims=True)) + 1e-06)
    return (stream * inverse_rms * section_gain[:, None, :]).astype(jnp.bfloat16)
```

```python
import functools
import math

import jax
import jax.numpy as jnp
from jax import lax
from jax.experimental import pallas as pl
from jax.experimental.pallas import tpu as pltpu
from jax.sharding import PartitionSpec as P

QUERY_HEADS = 64
KEY_VALUE_HEADS = 8
HEAD_SIZE = 128
BLOCK = 64
LONGEST_PROMPT = 512
CHUNKS = (64, 32, 32)
NEG = -1e30


def attention_kernel(first_row, order_ref, lengths_ref, vert_ref, slash_ref, q_ref, kv_ref, out_ref):
    rows = q_ref.shape[1]
    parts, part_rows = kv_ref.shape[0], kv_ref.shape[1]
    heads = q_ref.shape[2] // HEAD_SIZE
    keys = min(LONGEST_PROMPT + part_rows, parts * part_rows)
    factor = math.log2(math.e) / math.sqrt(HEAD_SIZE)
    part = order_ref[pl.program_id(0)]
    begin_part = jnp.clip(part - LONGEST_PROMPT // part_rows, 0, parts - keys // part_rows)
    begin = begin_part * part_rows
    query_first = part * part_rows + first_row
    query_pos = query_first + lax.broadcasted_iota(jnp.int32, (rows, 1), 0)
    own_start = jnp.zeros_like(query_pos)
    start = 0
    for p in range(lengths_ref.shape[0] - 1):
        start = start + lengths_ref[p]
        own_start = jnp.where(query_pos >= start, start, own_start)
    key_pos = begin + lax.broadcasted_iota(jnp.int32, (rows, keys), 1)
    token_bias = jnp.where((key_pos <= query_pos) & (key_pos >= own_start), 0.0, NEG)
    key_block = lax.shift_right_logical(
        begin + lax.broadcasted_iota(jnp.int32, (heads, keys), 1), int(math.log2(BLOCK))
    )
    offset = lax.shift_right_logical(query_first, int(math.log2(BLOCK))) - key_block
    hit = key_block == vert_ref[:, 0:1]
    for n in range(1, vert_ref.shape[1]):
        hit = hit | (key_block == vert_ref[:, n : n + 1])
    for n in range(slash_ref.shape[1]):
        hit = hit | (offset == slash_ref[:, n : n + 1])
    head_bias = jnp.where(hit, 0.0, NEG)
    key_value = kv_ref[pl.ds(begin_part, keys // part_rows)].reshape(keys, 2 * HEAD_SIZE)
    query = jnp.concatenate(
        [q_ref[0, :, h * HEAD_SIZE : (h + 1) * HEAD_SIZE] for h in range(heads)], axis=0
    )
    scores = lax.dot_general(
        query,
        key_value[:, :HEAD_SIZE],
        (((1,), (1,)), ((), ())),
        preferred_element_type=jnp.float32,
    )
    scores = scores.reshape(heads, rows, keys) + (token_bias[None] + head_bias[:, None, :])
    largest = jnp.max(scores, axis=-1, keepdims=True)
    weights = jnp.exp2((scores - largest) * factor)
    norm = jnp.sum(weights, axis=-1, keepdims=True)
    context = jnp.dot(
        weights.astype(jnp.bfloat16).reshape(heads * rows, keys),
        key_value[:, HEAD_SIZE:],
        preferred_element_type=jnp.float32,
    )
    context = (context.reshape(heads, rows, HEAD_SIZE) / norm).astype(jnp.bfloat16)
    for h in range(heads):
        out_ref[0, :, h * HEAD_SIZE : (h + 1) * HEAD_SIZE] = context[h]


def attention(first_row, rows, order, lengths, vert, slash, exchanged):
    parts, part_rows, width = exchanged.shape
    query_width = width - 2 * HEAD_SIZE
    return pl.pallas_call(
        functools.partial(attention_kernel, first_row),
        out_shape=jax.ShapeDtypeStruct((parts, rows, query_width), jnp.bfloat16),
        grid_spec=pltpu.PrefetchScalarGridSpec(
            num_scalar_prefetch=2,
            grid=(parts,),
            in_specs=[
                pl.BlockSpec(vert.shape, lambda n, order, lengths: (0, 0)),
                pl.BlockSpec(slash.shape, lambda n, order, lengths: (0, 0)),
                pl.BlockSpec(
                    (1, rows, query_width),
                    lambda n, order, lengths: (order[n], first_row // rows, 0),
                ),
                pl.BlockSpec(
                    (parts, part_rows, 2 * HEAD_SIZE),
                    lambda n, order, lengths: (0, 0, query_width // (2 * HEAD_SIZE)),
                ),
            ],
            out_specs=pl.BlockSpec(
                (1, rows, query_width), lambda n, order, lengths: (n, 0, 0)
            ),
        ),
        compiler_params=pltpu.CompilerParams(vmem_limit_bytes=32 << 20),
        name="attention",
    )(order, lengths, vert, slash, exchanged, exchanged)


def prefix_kernel(term_ref, out_ref):
    total = term_ref[0].astype(jnp.float32)
    out_ref[0] = term_ref[0]
    for layer in range(1, term_ref.shape[0]):
        total = total + term_ref[layer].astype(jnp.float32)
        out_ref[layer] = total.astype(jnp.bfloat16)


def prefix(terms):
    vmem = pl.BlockSpec(memory_space=pltpu.VMEM)
    return pl.pallas_call(
        prefix_kernel,
        out_shape=jax.ShapeDtypeStruct(terms.shape, jnp.bfloat16),
        in_specs=[vmem],
        out_specs=vmem,
        compiler_params=pltpu.CompilerParams(vmem_limit_bytes=32 << 20),
        name="prefix",
    )(terms)


def norm_kernel(residual_ref, sums_ref, gain_ref, out_ref):
    pieces, rows, width = sums_ref.shape
    square = jnp.zeros((rows, 1), jnp.float32)
    for n in range(pieces):
        stream = residual_ref[:, n * width : (n + 1) * width].astype(jnp.float32)
        stream = stream + sums_ref[n].astype(jnp.float32)
        square = square + jnp.sum(stream * stream, axis=-1, keepdims=True)
    inverse = lax.rsqrt(square / (pieces * width) + 1e-06)
    for n in range(pieces):
        place = slice(n * width, (n + 1) * width)
        stream = residual_ref[:, place].astype(jnp.float32) + sums_ref[n].astype(jnp.float32)
        out_ref[:, place] = (stream * inverse * gain_ref[:, place]).astype(jnp.bfloat16)


def normalize(residual, sums, gain):
    vmem = pl.BlockSpec(memory_space=pltpu.VMEM)
    return pl.pallas_call(
        norm_kernel,
        out_shape=jax.ShapeDtypeStruct(residual.shape, jnp.bfloat16),
        in_specs=[vmem, vmem, vmem],
        out_specs=vmem,
        compiler_params=pltpu.CompilerParams(vmem_limit_bytes=32 << 20),
        name="normalize",
    )(residual, sums, gain)


def add(first, second):
    return (first.astype(jnp.float32) + second.astype(jnp.float32)).astype(jnp.bfloat16)


def exchange_pairs(chips):
    def near(chip):
        return chip ^ 1

    def far(chip):
        return chips - 1 - chip

    cores = [(2 * x + c, 2 * x + 1 - c) for x in range(chips) for c in range(2)]
    first = [(2 * x + c, 2 * (near(x) if c == 0 else far(x)) + c) for x in range(chips) for c in range(2)]
    second = [(2 * x + c, 2 * (far(x) if c == 0 else near(x)) + c) for x in range(chips) for c in range(2)]
    return cores, first, second


def local(
    queries,
    layer_key_rows,
    layer_value_rows,
    vertical_blocks,
    slash_offsets,
    prompt_lengths,
    residual,
    out_weight,
    section_gain,
):
    parts = lax.axis_size("seq")
    layers = lax.axis_size("pipe")
    chips = parts // 2
    model = queries.shape[2]
    heads_here = QUERY_HEADS // parts
    place = lax.axis_index("seq")
    vert = lax.dynamic_slice_in_dim(vertical_blocks[0], place * heads_here, heads_here, 0)
    slash = lax.dynamic_slice_in_dim(slash_offsets[0], place * heads_here, heads_here, 0)

    def by_head(rows_in):
        return rows_in.reshape(rows_in.shape[0], parts, -1).transpose(1, 0, 2)

    exchanged = jnp.concatenate(
        [by_head(queries[0]), by_head(layer_key_rows[0]), by_head(layer_value_rows[0])], axis=2
    )
    exchanged = lax.all_to_all(exchanged, "seq", 0, 0)

    chip, core = place // 2, place % 2
    near, far = chip ^ 1, chips - 1 - chip
    first_chip = jnp.where(core == 0, near, far)
    second_chip = jnp.where(core == 0, far, near)
    across = chips - 1 - near
    order = jnp.stack(
        [
            2 * chip + 1 - core,
            2 * first_chip + 1 - core,
            2 * second_chip + 1 - core,
            2 * across + 1 - core,
            2 * chip + core,
            2 * second_chip + core,
            2 * first_chip + core,
            2 * across + core,
        ]
    ).astype(jnp.int32)
    to_core, to_first, to_second = exchange_pairs(chips)

    outs = []
    first = 0
    for chunk in CHUNKS:
        context = attention(first, chunk, order, prompt_lengths, vert, slash, exchanged)
        context = context.reshape(2, chips * chunk, model // parts)

        def project(rows_in):
            return jnp.dot(
                rows_in, out_weight[0], preferred_element_type=jnp.float32
            ).astype(jnp.bfloat16)

        arrived = lax.ppermute(project(context[0]), "seq", to_core)
        kept = project(context[1])
        half = chips * chunk // 2
        arrived_first = lax.ppermute(add(kept[half:], arrived[half:]), "seq", to_first)
        kept = add(kept[:half], arrived[:half])
        quarter = half // 2
        arrived_second = lax.ppermute(
            add(kept[quarter:], arrived_first[quarter:]), "seq", to_second
        )
        term = add(add(kept[:quarter], arrived_first[:quarter]), arrived_second)
        term = term.reshape(chunk, layers, model // layers).transpose(1, 0, 2)
        sums = prefix(lax.all_to_all(term, "pipe", 0, 0))
        sums = lax.all_to_all(sums, "pipe", 0, 0)
        outs.append(normalize(residual[first : first + chunk], sums, section_gain))
        first += chunk
    return jnp.concatenate(outs, axis=0)[None]


def solution(mesh):
    placed = (
        P("pipe", "seq", None),
        P("pipe", "seq", None),
        P("pipe", "seq", None),
        P("pipe", None, None),
        P("pipe", None, None),
        P(),
        P("seq", None),
        P("pipe", "seq", None),
        P("pipe", None),
    )
    return jax.shard_map(
        local, mesh=mesh, in_specs=placed, out_specs=P("pipe", "seq", None), check_vma=False
    )
```

```python
import functools
import math

import jax
import jax.numpy as jnp
from jax import lax
from jax.experimental import pallas as pl
from jax.experimental.pallas import tpu as pltpu
from jax.sharding import PartitionSpec as P

QUERY_HEADS = 64
HEAD_SIZE = 128
BLOCK = 64
LONGEST_PROMPT = 512
CHUNKS = (((0, 48),), ((64, 48),), ((48, 16), (112, 16)))
GROUP = 32
PACK_STEPS = 2
ROW_TILE = 16
LEAD = 48
PIECES = 4
COLUMNS = 1024
AHEAD = 4
FETCHES = 2
NEG = -1e30
COST = pl.CostEstimate(flops=0, transcendentals=0, bytes_accessed=0)
PARAMS = pltpu.CompilerParams(vmem_limit_bytes=16 << 20)


def pack_kernel(q_ref, k_ref, v_ref, first_ref, rest_ref):
    dests, lead_rows, width = first_ref.shape
    rows = lead_rows - GROUP
    for dest in range(dests):
        place = slice(dest * width, (dest + 1) * width)
        first_ref[dest, :rows] = q_ref[:rows, place]
        rest_ref[dest] = q_ref[rows:, place]
        column = 0
        for ref in (k_ref, v_ref):
            for begin in range(0, ref.shape[0], GROUP):
                first_ref[dest, rows:, column : column + HEAD_SIZE] = ref[
                    begin : begin + GROUP, dest * HEAD_SIZE : (dest + 1) * HEAD_SIZE
                ]
                column += HEAD_SIZE


def pack(parts, rows, queries, keys, values):
    tokens, model = queries.shape
    width = model // parts
    dests = parts // PACK_STEPS
    return pl.pallas_call(
        pack_kernel,
        out_shape=(
            pltpu.HBM((parts, rows + GROUP, width), jnp.bfloat16),
            pltpu.HBM((parts, tokens - rows, width), jnp.bfloat16),
        ),
        grid=(PACK_STEPS,),
        in_specs=[
            pl.BlockSpec((tokens, dests * width), lambda n: (0, n)),
            pl.BlockSpec((tokens, dests * HEAD_SIZE), lambda n: (0, n)),
            pl.BlockSpec((tokens, dests * HEAD_SIZE), lambda n: (0, n)),
        ],
        out_specs=(
            pl.BlockSpec((dests, rows + GROUP, width), lambda n: (n, 0, 0)),
            pl.BlockSpec((dests, tokens - rows, width), lambda n: (n, 0, 0)),
        ),
        compiler_params=PARAMS,
        cost_estimate=COST,
        name="pack",
    )(queries, keys, values)


def attend(queries, key, value, bias):
    heads, rows, _ = bias.shape
    factor = math.log2(math.e) / math.sqrt(HEAD_SIZE)
    scores = lax.dot_general(
        queries, key, (((1,), (1,)), ((), ())), preferred_element_type=jnp.float32
    )
    scores = scores.reshape(bias.shape) + bias
    largest = jnp.max(scores, axis=-1, keepdims=True)
    weights = jnp.exp2((scores - largest) * factor)
    norm = jnp.sum(weights, axis=-1, keepdims=True)
    context = jnp.dot(
        weights.astype(jnp.bfloat16).reshape(heads * rows, -1),
        value,
        preferred_element_type=jnp.float32,
    )
    return (context.reshape(heads, rows, HEAD_SIZE) / norm).astype(jnp.bfloat16)


def gather_keys(kv_ref, kv_scratch, part_rows):
    parts, lead_rows = kv_ref.shape[0], kv_ref.shape[1]
    groups = part_rows // GROUP
    for part in range(parts):
        for group in range(groups):
            begin = part * part_rows + group * GROUP
            for which in range(2):
                column = (which * groups + group) * HEAD_SIZE
                kv_scratch[begin : begin + GROUP, which * HEAD_SIZE : (which + 1) * HEAD_SIZE] = kv_ref[
                    part, lead_rows - GROUP :, column : column + HEAD_SIZE
                ]


def attend_part(
    lead, segments, part, parts, part_rows, lengths_ref, vert_ref, slash_ref, q_ref, kv_scratch, store
):
    heads = vert_ref.shape[0]
    lowest = jnp.int32(0)
    starts = []
    start = 0
    for p in range(lengths_ref.shape[0] - 1):
        start = start + lengths_ref[p]
        starts.append(start)
        lowest = jnp.where(part * part_rows + segments[0][0] >= start, start, lowest)
    shift = int(math.log2(BLOCK))
    rest = lead if segments[0][0] >= lead else 0
    queries = jnp.concatenate(
        [
            q_ref[0, first - rest : first - rest + count, h * HEAD_SIZE : (h + 1) * HEAD_SIZE]
            for h in range(heads)
            for first, count in segments
        ],
        axis=0,
    )
    needed = part + 1 - lax.div(lowest, part_rows)

    def window(count):
        keys = count * part_rows
        begin_part = jnp.clip(part + 1 - count, 0, parts - count)
        begin = pl.multiple_of(begin_part * part_rows, part_rows)
        key_block = lax.shift_right_logical(
            begin + lax.broadcasted_iota(jnp.int32, (heads, keys), 1), shift
        )
        vertical = key_block == vert_ref[:, 0:1]
        for n in range(1, vert_ref.shape[1]):
            vertical = vertical | (key_block == vert_ref[:, n : n + 1])
        biases = []
        for first, count in segments:
            query_first = part * part_rows + first
            query_pos = query_first + lax.broadcasted_iota(jnp.int32, (count, 1), 0)
            own_start = jnp.zeros_like(query_pos)
            for start in starts:
                own_start = jnp.where(query_pos >= start, start, own_start)
            key_pos = begin + lax.broadcasted_iota(jnp.int32, (count, keys), 1)
            token_bias = jnp.where((key_pos <= query_pos) & (key_pos >= own_start), 0.0, NEG)
            offset = lax.shift_right_logical(query_first, shift) - key_block
            hit = vertical
            for n in range(slash_ref.shape[1]):
                hit = hit | (offset == slash_ref[:, n : n + 1])
            head_bias = jnp.where(hit, 0.0, NEG)
            biases.append(token_bias[None] + head_bias[:, None, :])
        key_value = kv_scratch[pl.ds(begin, keys)]
        context = attend(
            queries,
            key_value[:, :HEAD_SIZE],
            key_value[:, HEAD_SIZE:],
            biases[0] if len(biases) == 1 else jnp.concatenate(biases, axis=1),
        )
        for h in range(heads):
            store(h, context[h])

    counts = [2, 3, min(LONGEST_PROMPT // part_rows + 1, parts)]
    for n, count in enumerate(counts):
        fits = needed > counts[n - 1] if n else needed <= count
        if 0 < n < len(counts) - 1:
            fits = fits & (needed <= count)
        pl.when(fits)(functools.partial(window, count))


def context_kernel(
    lead, segments, part_rows, order_ref, lengths_ref, vert_ref, slash_ref, q_ref, kv_ref, out_ref, kv_scratch
):
    step = pl.program_id(0)
    pl.when(step == 0)(lambda: gather_keys(kv_ref, kv_scratch, part_rows))

    def store(head, rows):
        out_ref[0, :, head * HEAD_SIZE : (head + 1) * HEAD_SIZE] = rows

    attend_part(
        lead, segments, order_ref[step], kv_ref.shape[0], part_rows, lengths_ref, vert_ref, slash_ref,
        q_ref, kv_scratch, store,
    )


def attention(lead, segments, part_rows, order, lengths, vert, slash, queries, key_value):
    parts, query_rows = queries.shape[:2]
    blocks = order.shape[0]
    rows = sum(count for _, count in segments)
    width = vert.shape[0] * HEAD_SIZE
    return pl.pallas_call(
        functools.partial(context_kernel, lead, segments, part_rows),
        out_shape=jax.ShapeDtypeStruct((blocks, rows, width), jnp.bfloat16),
        grid_spec=pltpu.PrefetchScalarGridSpec(
            num_scalar_prefetch=2,
            grid=(blocks,),
            in_specs=[
                pl.BlockSpec(vert.shape, lambda n, order, lengths: (0, 0)),
                pl.BlockSpec(slash.shape, lambda n, order, lengths: (0, 0)),
                pl.BlockSpec((1, query_rows, width), lambda n, order, lengths: (order[n], 0, 0)),
                pl.BlockSpec(key_value.shape, lambda n, order, lengths: (0, 0, 0)),
            ],
            out_specs=pl.BlockSpec((1, rows, width), lambda n, order, lengths: (n, 0, 0)),
            scratch_shapes=[pltpu.VMEM((parts * part_rows, 2 * HEAD_SIZE), jnp.bfloat16)],
        ),
        compiler_params=PARAMS,
        cost_estimate=COST,
        name="attention",
    )(order, lengths, vert, slash, queries, key_value)


def project_kernel(context_ref, weight_ref, *refs):
    *send_refs, keep_ref, weight_scratch, sems = refs
    tile = pl.program_id(0)
    tiles = weight_scratch.shape[0]

    def fetch(number):
        rows = weight_ref.shape[0] // FETCHES
        return [
            pltpu.make_async_copy(
                weight_ref.at[pl.ds(n * rows, rows), pl.ds(number * COLUMNS, COLUMNS)],
                weight_scratch.at[number, pl.ds(n * rows, rows)],
                sems.at[number, n],
            )
            for n in range(FETCHES)
        ]

    @pl.when(tile == 0)
    def _():
        for number in range(AHEAD):
            for copy in fetch(number):
                copy.start()

    @pl.when(tile + AHEAD < tiles)
    def _():
        for copy in fetch(tile + AHEAD):
            copy.start()

    for copy in fetch(tile):
        copy.wait()
    term = jnp.dot(
        context_ref[...].reshape(-1, context_ref.shape[2]),
        weight_scratch[tile],
        preferred_element_type=jnp.float32,
    ).astype(jnp.bfloat16)
    half = keep_ref.shape[0]
    keep_ref[...] = term[half:]
    per_piece = pl.num_programs(0) // len(send_refs)
    for piece, send_ref in enumerate(send_refs):

        @pl.when((tile >= piece * per_piece) & (tile < (piece + 1) * per_piece))
        def _():
            send_ref[...] = term[:half]


def project(context, weight):
    blocks, block_rows, width = context.shape
    half = blocks * block_rows // 2
    model = weight.shape[1]
    tiles = model // COLUMNS
    per_piece = tiles // PIECES

    def out_spec(piece, count):
        return pl.BlockSpec((half, COLUMNS), lambda n: (0, jnp.clip(n - piece * count, 0, count - 1)))

    return pl.pallas_call(
        project_kernel,
        out_shape=tuple(
            jax.ShapeDtypeStruct((half, model // PIECES), jnp.bfloat16) for _ in range(PIECES)
        )
        + (pltpu.HBM((half, model), jnp.bfloat16),),
        grid=(tiles,),
        in_specs=[
            pl.BlockSpec(context.shape, lambda n: (0, 0, 0)),
            pl.BlockSpec(memory_space=pl.ANY),
        ],
        out_specs=tuple(out_spec(piece, per_piece) for piece in range(PIECES)) + (out_spec(0, tiles),),
        scratch_shapes=[
            pltpu.VMEM((tiles, width, COLUMNS), jnp.bfloat16),
            pltpu.SemaphoreType.DMA((tiles, FETCHES)),
        ],
        compiler_params=pltpu.CompilerParams(vmem_limit_bytes=34 << 20),
        cost_estimate=COST,
        name="project",
    )(context, weight)


def join_kernel(kept_ref, *refs):
    *arrived_refs, keep_ref, send_ref = refs
    rows = keep_ref.shape[0]
    for piece, arrived_ref in enumerate(arrived_refs):

        @pl.when(pl.program_id(0) == piece)
        def _():
            total = kept_ref[...].astype(jnp.float32) + arrived_ref[...].astype(jnp.float32)
            total = total.astype(jnp.bfloat16)
            keep_ref[...] = total[:rows]
            send_ref[...] = total[rows:]


def join(kept, arrived):
    rows, model = kept.shape
    pieces = len(arrived)
    columns = model // pieces
    half = pltpu.HBM((rows // 2, model), jnp.bfloat16)
    half_spec = pl.BlockSpec((rows // 2, columns), lambda n: (0, n))
    whole = pl.BlockSpec((rows, columns), lambda n: (0, 0))
    return pl.pallas_call(
        join_kernel,
        out_shape=(half, half),
        grid=(pieces,),
        in_specs=[pl.BlockSpec((rows, columns), lambda n: (0, n))] + [whole] * pieces,
        out_specs=(half_spec, half_spec),
        compiler_params=PARAMS,
        cost_estimate=COST,
        name="join",
    )(kept, *arrived)


def finish_kernel(*refs):
    *term_refs, out_ref = refs
    layers, _, width = out_ref.shape
    begin = 0
    for kept_ref, first_ref, second_ref in zip(term_refs[::3], term_refs[1::3], term_refs[2::3]):
        rows = second_ref.shape[0]
        total = kept_ref[...].astype(jnp.float32) + first_ref[...].astype(jnp.float32)
        total = (total + second_ref[...].astype(jnp.float32)).astype(jnp.bfloat16)
        for n in range(layers):
            out_ref[n, begin : begin + rows] = total[:, n * width : (n + 1) * width]
        begin += rows


def finish(layers, *chunks):
    model = chunks[0][2].shape[1]
    width = model // layers
    group = layers // 2
    operands, in_specs = [], []
    for kept, first, second in chunks:
        rows = second.shape[0]
        operands += [kept, first, second]
        in_specs += [pl.BlockSpec((rows, group * width), lambda n: (0, n))] * 3
    rows = sum(second.shape[0] for _, _, second in chunks)
    return pl.pallas_call(
        finish_kernel,
        out_shape=pltpu.HBM((layers, rows, width), jnp.bfloat16),
        grid=(layers // group,),
        in_specs=in_specs,
        out_specs=pl.BlockSpec((group, rows, width), lambda n: (n, 0, 0)),
        compiler_params=PARAMS,
        cost_estimate=COST,
        name="finish",
    )(*operands)


def prefix_kernel(term_ref, out_ref):
    total = term_ref[0].astype(jnp.float32)
    out_ref[0] = term_ref[0]
    for layer in range(1, term_ref.shape[0]):
        total = total + term_ref[layer].astype(jnp.float32)
        out_ref[layer] = total.astype(jnp.bfloat16)


def prefix(terms):
    layers, rows, width = terms.shape
    spec = pl.BlockSpec((layers, rows // 2, width), lambda n: (0, n, 0))
    return pl.pallas_call(
        prefix_kernel,
        out_shape=pltpu.HBM(terms.shape, jnp.bfloat16),
        grid=(2,),
        in_specs=[spec],
        out_specs=spec,
        compiler_params=PARAMS,
        cost_estimate=COST,
        name="prefix",
    )(terms)


def norm_kernel(residual_ref, sums_ref, gain_ref, *refs):
    out_ref = refs[-1]
    pieces, rows, width = sums_ref.shape
    square = jnp.zeros((rows, 1), jnp.float32)
    for n in range(pieces):
        stream = residual_ref[:, n * width : (n + 1) * width].astype(jnp.float32)
        stream = stream + sums_ref[n].astype(jnp.float32)
        square = square + jnp.sum(stream * stream, axis=-1, keepdims=True)
    inverse = lax.rsqrt(square / (pieces * width) + 1e-06)
    for n in range(pieces):
        place = slice(n * width, (n + 1) * width)
        stream = residual_ref[:, place].astype(jnp.float32) + sums_ref[n].astype(jnp.float32)
        out_ref[:, place] = (stream * inverse * gain_ref[:, place]).astype(jnp.bfloat16)


def normalize(segments, residual, sums, gain, filled):
    model = residual.shape[1]
    tiles = [
        (first + begin) // ROW_TILE for first, count in segments for begin in range(0, count, ROW_TILE)
    ]

    def row_tile(n):
        tile = jnp.int32(tiles[0])
        for place, number in enumerate(tiles[1:], 1):
            tile = jnp.where(n == place, number, tile)
        return tile

    row_spec = pl.BlockSpec((ROW_TILE, model), lambda n: (row_tile(n), 0))
    layers, _, width = sums.shape
    in_specs = [
        row_spec,
        pl.BlockSpec((layers, ROW_TILE, width), lambda n: (0, n, 0)),
        pl.BlockSpec(gain.shape, lambda n: (0, 0)),
    ]
    operands = [residual, sums, gain]
    aliases = {}
    if filled is not None:
        in_specs.append(pl.BlockSpec(memory_space=pl.ANY))
        operands.append(filled)
        aliases = {3: 0}
    return pl.pallas_call(
        norm_kernel,
        out_shape=jax.ShapeDtypeStruct(residual.shape, jnp.bfloat16),
        grid=(len(tiles),),
        in_specs=in_specs,
        out_specs=row_spec,
        input_output_aliases=aliases,
        compiler_params=PARAMS,
        cost_estimate=COST,
        name="normalize",
    )(*operands)


def add(first, second):
    return (first.astype(jnp.float32) + second.astype(jnp.float32)).astype(jnp.bfloat16)


def after(value, *others):
    return lax.optimization_barrier((value, *others))[0]


def exchange_pairs(chips):
    def near(chip):
        return chip ^ 1

    def far(chip):
        return chips - 1 - chip

    every = [(x, c) for x in range(chips) for c in range(2)]
    cores = [(2 * x + c, 2 * x + 1 - c) for x, c in every]
    first = [(2 * x + c, 2 * (near(x) if c == 0 else far(x)) + c) for x, c in every]
    second = [(2 * x + c, 2 * (far(x) if c == 0 else near(x)) + c) for x, c in every]
    return cores, first, second


def local(
    queries,
    layer_key_rows,
    layer_value_rows,
    vertical_blocks,
    slash_offsets,
    prompt_lengths,
    residual,
    out_weight,
    section_gain,
):
    parts = lax.axis_size("seq")
    layers = lax.axis_size("pipe")
    chips = parts // 2
    tokens, model = queries.shape[1:]
    heads_here = QUERY_HEADS // parts
    place = lax.axis_index("seq")
    vert = lax.dynamic_slice_in_dim(vertical_blocks[0], place * heads_here, heads_here, 0)
    slash = lax.dynamic_slice_in_dim(slash_offsets[0], place * heads_here, heads_here, 0)

    lead = LEAD
    def in_hbm(array):
        return pltpu.with_memory_space_constraint(array, pltpu.HBM)

    lead_block, rest_block = pack(
        parts, lead, in_hbm(queries[0]), in_hbm(layer_key_rows[0]), in_hbm(layer_value_rows[0])
    )
    lead_block = lax.all_to_all(lead_block, "seq", 0, 0)
    rest_block = after(rest_block, lead_block)
    rest_block = lax.all_to_all(rest_block, "seq", 0, 0)

    chip, core = place // 2, place % 2
    near, far = chip ^ 1, chips - 1 - chip
    first_chip = jnp.where(core == 0, near, far)
    second_chip = jnp.where(core == 0, far, near)
    across = chips - 1 - near
    send = jnp.stack([chip, first_chip, second_chip, across]) * 2 + (1 - core)
    keep = jnp.stack([chip, second_chip, first_chip, across]) * 2 + core
    send, keep = send.astype(jnp.int32), keep.astype(jnp.int32)
    to_core, to_first, to_second = exchange_pairs(chips)

    weight = in_hbm(out_weight[0])
    order = jnp.concatenate([send, keep])

    def attend_chunk(segments, *others):
        source = lead_block if segments[0][0] < lead else rest_block
        return attention(
            lead, segments, tokens, after(order, *others), prompt_lengths, vert, slash, source, lead_block
        )

    def project_chunk(context, *others):
        *sent, kept = project(after(context, *others), weight)
        return kept, [lax.ppermute(piece, "seq", to_core) for piece in sent], sent[0]

    def reduce_next(kept, arrived_first, *others):
        rows = kept.shape[0] // 2
        to_send = after(add(kept[rows:], arrived_first[rows:]), *others)
        return lax.ppermute(to_send, "seq", to_second), to_send

    chunk_a, chunk_b, chunk_c = CHUNKS
    context_a = attend_chunk(chunk_a)
    kept_a, pieces_a, token_a = project_chunk(context_a)
    context_b = attend_chunk(chunk_b, token_a)
    kept_a, sent_a = join(after(kept_a, context_b), pieces_a)
    first_a = lax.ppermute(sent_a, "seq", to_first)
    kept_b, pieces_b, token_b = project_chunk(context_b, sent_a)
    context_c = attend_chunk(chunk_c, token_b)
    second_a, next_a = reduce_next(kept_a, first_a, context_c)
    kept_c, pieces_c, token_c = project_chunk(context_c, next_a)
    kept_b, sent_b = join(after(kept_b, token_c, second_a), pieces_b)
    first_b = lax.ppermute(sent_b, "seq", to_first)
    kept_c, sent_c = join(kept_c, pieces_c)
    first_c = lax.ppermute(sent_c, "seq", to_first)
    term_a = finish(layers, (kept_a, first_a, after(second_a, sent_c)))
    terms_a = lax.all_to_all(term_a, "pipe", 0, 0)
    second_b, next_b = reduce_next(kept_b, first_b, term_a)
    prefix_a = prefix(after(terms_a, next_b))
    sums_a = lax.all_to_all(prefix_a, "pipe", 0, 0)
    second_c, next_c = reduce_next(kept_c, first_c, prefix_a)
    term_bc = finish(layers, (kept_b, first_b, second_b), (kept_c, first_c, second_c))
    terms_bc = lax.all_to_all(after(term_bc, sums_a), "pipe", 0, 0)
    sums_bc = lax.all_to_all(prefix(terms_bc), "pipe", 0, 0)
    residual = in_hbm(residual)
    out = None
    for segments, sums in ((chunk_a, sums_a), (chunk_b + chunk_c, sums_bc)):
        out = normalize(segments, residual, sums, section_gain, out)
    return out[None]


def solution(mesh):
    placed = (
        P("pipe", "seq", None),
        P("pipe", "seq", None),
        P("pipe", "seq", None),
        P("pipe", None, None),
        P("pipe", None, None),
        P(),
        P("seq", None),
        P("pipe", "seq", None),
        P("pipe", None),
    )
    return jax.shard_map(
        local, mesh=mesh, in_specs=placed, out_specs=P("pipe", "seq", None), check_vma=False
    )
```

```python
import functools
import math

import jax
import jax.numpy as jnp
from jax import lax
from jax.experimental import pallas as pl
from jax.experimental.pallas import tpu as pltpu
from jax.sharding import PartitionSpec as P

QUERY_HEADS = 64
HEAD_SIZE = 128
BLOCK = 64
LONGEST_PROMPT = 512
CHUNKS = (((0, 48),), ((64, 48),), ((48, 16), (112, 16)))
GROUP = 32
PACK_STEPS = 2
ROW_TILE = 16
LEAD = 48
PIECES = 4
COLUMNS = 1024
AHEAD = 4
FETCHES = 2
NEG = -1e30
COST = pl.CostEstimate(flops=0, transcendentals=0, bytes_accessed=0)
PARAMS = pltpu.CompilerParams(vmem_limit_bytes=16 << 20)


def pack_lead_kernel(q_ref, k_ref, v_ref, out_ref):
    dests, lead_rows, width = out_ref.shape
    rows = lead_rows - GROUP
    for dest in range(dests):
        out_ref[dest, :rows] = q_ref[:, dest * width : (dest + 1) * width]
        column = 0
        for ref in (k_ref, v_ref):
            for begin in range(0, ref.shape[0], GROUP):
                out_ref[dest, rows:, column : column + HEAD_SIZE] = ref[
                    begin : begin + GROUP, dest * HEAD_SIZE : (dest + 1) * HEAD_SIZE
                ]
                column += HEAD_SIZE


def pack_lead(parts, rows, queries, keys, values):
    tokens, model = queries.shape
    width = model // parts
    dests = parts // PACK_STEPS
    return pl.pallas_call(
        pack_lead_kernel,
        out_shape=pltpu.HBM((parts, rows + GROUP, width), jnp.bfloat16),
        grid=(PACK_STEPS,),
        in_specs=[
            pl.BlockSpec((rows, dests * width), lambda n: (0, n)),
            pl.BlockSpec((tokens, dests * HEAD_SIZE), lambda n: (0, n)),
            pl.BlockSpec((tokens, dests * HEAD_SIZE), lambda n: (0, n)),
        ],
        out_specs=pl.BlockSpec((dests, rows + GROUP, width), lambda n: (n, 0, 0)),
        compiler_params=PARAMS,
        cost_estimate=COST,
        name="pack_lead",
    )(queries, keys, values)


def pack_rest_kernel(q_ref, out_ref):
    dests, rows, width = out_ref.shape
    for dest in range(dests):
        out_ref[dest] = q_ref[q_ref.shape[0] - rows :, dest * width : (dest + 1) * width]


def pack_rest(parts, rows, queries):
    tokens, model = queries.shape
    width = model // parts
    dests = parts // PACK_STEPS
    return pl.pallas_call(
        pack_rest_kernel,
        out_shape=pltpu.HBM((parts, tokens - rows, width), jnp.bfloat16),
        grid=(PACK_STEPS,),
        in_specs=[pl.BlockSpec((tokens, dests * width), lambda n: (0, n))],
        out_specs=pl.BlockSpec((dests, tokens - rows, width), lambda n: (n, 0, 0)),
        compiler_params=PARAMS,
        cost_estimate=COST,
        name="pack_rest",
    )(queries)


def attend(queries, key, value, bias):
    heads, rows, _ = bias.shape
    factor = math.log2(math.e) / math.sqrt(HEAD_SIZE)
    scores = lax.dot_general(
        queries, key, (((1,), (1,)), ((), ())), preferred_element_type=jnp.float32
    )
    scores = scores.reshape(bias.shape) + bias
    largest = jnp.max(scores, axis=-1, keepdims=True)
    weights = jnp.exp2((scores - largest) * factor)
    norm = jnp.sum(weights, axis=-1, keepdims=True)
    context = jnp.dot(
        weights.astype(jnp.bfloat16).reshape(heads * rows, -1),
        value,
        preferred_element_type=jnp.float32,
    )
    return (context.reshape(heads, rows, HEAD_SIZE) / norm).astype(jnp.bfloat16)


def gather_keys(kv_ref, kv_scratch, part_rows):
    parts, lead_rows = kv_ref.shape[0], kv_ref.shape[1]
    groups = part_rows // GROUP
    for part in range(parts):
        for group in range(groups):
            begin = part * part_rows + group * GROUP
            for which in range(2):
                column = (which * groups + group) * HEAD_SIZE
                kv_scratch[begin : begin + GROUP, which * HEAD_SIZE : (which + 1) * HEAD_SIZE] = kv_ref[
                    part, lead_rows - GROUP :, column : column + HEAD_SIZE
                ]


def attend_part(
    lead, segments, part, parts, part_rows, lengths_ref, vert_ref, slash_ref, q_ref, kv_scratch, store
):
    heads = vert_ref.shape[0]
    lowest = jnp.int32(0)
    starts = []
    start = 0
    for p in range(lengths_ref.shape[0] - 1):
        start = start + lengths_ref[p]
        starts.append(start)
        lowest = jnp.where(part * part_rows + segments[0][0] >= start, start, lowest)
    shift = int(math.log2(BLOCK))
    rest = lead if segments[0][0] >= lead else 0
    queries = jnp.concatenate(
        [
            q_ref[0, first - rest : first - rest + count, h * HEAD_SIZE : (h + 1) * HEAD_SIZE]
            for h in range(heads)
            for first, count in segments
        ],
        axis=0,
    )
    needed = part + 1 - lax.div(lowest, part_rows)

    def window(count):
        keys = count * part_rows
        begin_part = jnp.clip(part + 1 - count, 0, parts - count)
        begin = pl.multiple_of(begin_part * part_rows, part_rows)
        key_block = lax.shift_right_logical(
            begin + lax.broadcasted_iota(jnp.int32, (heads, keys), 1), shift
        )
        vertical = key_block == vert_ref[:, 0:1]
        for n in range(1, vert_ref.shape[1]):
            vertical = vertical | (key_block == vert_ref[:, n : n + 1])
        biases = []
        for first, count in segments:
            query_first = part * part_rows + first
            query_pos = query_first + lax.broadcasted_iota(jnp.int32, (count, 1), 0)
            own_start = jnp.zeros_like(query_pos)
            for start in starts:
                own_start = jnp.where(query_pos >= start, start, own_start)
            key_pos = begin + lax.broadcasted_iota(jnp.int32, (count, keys), 1)
            token_bias = jnp.where((key_pos <= query_pos) & (key_pos >= own_start), 0.0, NEG)
            offset = lax.shift_right_logical(query_first, shift) - key_block
            hit = vertical
            for n in range(slash_ref.shape[1]):
                hit = hit | (offset == slash_ref[:, n : n + 1])
            head_bias = jnp.where(hit, 0.0, NEG)
            biases.append(token_bias[None] + head_bias[:, None, :])
        key_value = kv_scratch[pl.ds(begin, keys)]
        context = attend(
            queries,
            key_value[:, :HEAD_SIZE],
            key_value[:, HEAD_SIZE:],
            biases[0] if len(biases) == 1 else jnp.concatenate(biases, axis=1),
        )
        for h in range(heads):
            store(h, context[h])

    counts = [2, 3, min(LONGEST_PROMPT // part_rows + 1, parts)]
    for n, count in enumerate(counts):
        fits = needed > counts[n - 1] if n else needed <= count
        if 0 < n < len(counts) - 1:
            fits = fits & (needed <= count)
        pl.when(fits)(functools.partial(window, count))


def context_kernel(
    lead, segments, part_rows, order_ref, lengths_ref, vert_ref, slash_ref, q_ref, kv_ref, out_ref, kv_scratch
):
    step = pl.program_id(0)
    pl.when(step == 0)(lambda: gather_keys(kv_ref, kv_scratch, part_rows))

    def store(head, rows):
        out_ref[0, :, head * HEAD_SIZE : (head + 1) * HEAD_SIZE] = rows

    attend_part(
        lead, segments, order_ref[step], kv_ref.shape[0], part_rows, lengths_ref, vert_ref, slash_ref,
        q_ref, kv_scratch, store,
    )


def attention(lead, segments, part_rows, order, lengths, vert, slash, queries, key_value):
    parts, query_rows = queries.shape[:2]
    blocks = order.shape[0]
    rows = sum(count for _, count in segments)
    width = vert.shape[0] * HEAD_SIZE
    return pl.pallas_call(
        functools.partial(context_kernel, lead, segments, part_rows),
        out_shape=jax.ShapeDtypeStruct((blocks, rows, width), jnp.bfloat16),
        grid_spec=pltpu.PrefetchScalarGridSpec(
            num_scalar_prefetch=2,
            grid=(blocks,),
            in_specs=[
                pl.BlockSpec(vert.shape, lambda n, order, lengths: (0, 0)),
                pl.BlockSpec(slash.shape, lambda n, order, lengths: (0, 0)),
                pl.BlockSpec((1, query_rows, width), lambda n, order, lengths: (order[n], 0, 0)),
                pl.BlockSpec(key_value.shape, lambda n, order, lengths: (0, 0, 0)),
            ],
            out_specs=pl.BlockSpec((1, rows, width), lambda n, order, lengths: (n, 0, 0)),
            scratch_shapes=[pltpu.VMEM((parts * part_rows, 2 * HEAD_SIZE), jnp.bfloat16)],
        ),
        compiler_params=PARAMS,
        cost_estimate=COST,
        name="attention",
    )(order, lengths, vert, slash, queries, key_value)


def project_kernel(context_ref, weight_ref, *refs):
    *send_refs, keep_ref, weight_scratch, sems = refs
    tile = pl.program_id(0)
    tiles = pl.num_programs(0)

    def slot(number):
        return lax.rem(number, weight_scratch.shape[0])

    def fetch(number):
        rows = weight_ref.shape[0] // FETCHES
        return [
            pltpu.make_async_copy(
                weight_ref.at[pl.ds(n * rows, rows), pl.ds(number * COLUMNS, COLUMNS)],
                weight_scratch.at[slot(number), pl.ds(n * rows, rows)],
                sems.at[slot(number), n],
            )
            for n in range(FETCHES)
        ]

    @pl.when(tile == 0)
    def _():
        for number in range(AHEAD):
            for copy in fetch(jnp.int32(number)):
                copy.start()

    @pl.when(tile + AHEAD < tiles)
    def _():
        for copy in fetch(tile + AHEAD):
            copy.start()

    for copy in fetch(tile):
        copy.wait()
    term = jnp.dot(
        context_ref[...].reshape(-1, context_ref.shape[2]),
        weight_scratch[slot(tile)],
        preferred_element_type=jnp.float32,
    ).astype(jnp.bfloat16)
    half = keep_ref.shape[0]
    keep_ref[...] = term[half:]
    per_piece = pl.num_programs(0) // len(send_refs)
    for piece, send_ref in enumerate(send_refs):

        @pl.when((tile >= piece * per_piece) & (tile < (piece + 1) * per_piece))
        def _():
            send_ref[...] = term[:half]


def project(context, weight):
    blocks, block_rows, width = context.shape
    half = blocks * block_rows // 2
    model = weight.shape[1]
    tiles = model // COLUMNS
    per_piece = tiles // PIECES

    def out_spec(piece, count):
        return pl.BlockSpec((half, COLUMNS), lambda n: (0, jnp.clip(n - piece * count, 0, count - 1)))

    return pl.pallas_call(
        project_kernel,
        out_shape=tuple(
            pltpu.VMEM((half, model // PIECES), jnp.bfloat16) for _ in range(PIECES)
        )
        + (pltpu.HBM((half, model), jnp.bfloat16),),
        grid=(tiles,),
        in_specs=[
            pl.BlockSpec(context.shape, lambda n: (0, 0, 0)),
            pl.BlockSpec(memory_space=pl.ANY),
        ],
        out_specs=tuple(out_spec(piece, per_piece) for piece in range(PIECES)) + (out_spec(0, tiles),),
        scratch_shapes=[
            pltpu.VMEM((AHEAD + 1, width, COLUMNS), jnp.bfloat16),
            pltpu.SemaphoreType.DMA((AHEAD + 1, FETCHES)),
        ],
        compiler_params=pltpu.CompilerParams(vmem_limit_bytes=24 << 20),
        cost_estimate=COST,
        name="project",
    )(context, weight)


def join_kernel(kept_ref, *refs):
    *arrived_refs, keep_ref, send_ref = refs
    rows = keep_ref.shape[0]
    for piece, arrived_ref in enumerate(arrived_refs):

        @pl.when(pl.program_id(0) == piece)
        def _():
            total = kept_ref[...].astype(jnp.float32) + arrived_ref[...].astype(jnp.float32)
            total = total.astype(jnp.bfloat16)
            keep_ref[...] = total[:rows]
            send_ref[...] = total[rows:]


def join(kept, arrived):
    rows, model = kept.shape
    pieces = len(arrived)
    columns = model // pieces
    half = pltpu.HBM((rows // 2, model), jnp.bfloat16)
    half_spec = pl.BlockSpec((rows // 2, columns), lambda n: (0, n))
    whole = pl.BlockSpec((rows, columns), lambda n: (0, 0))
    return pl.pallas_call(
        join_kernel,
        out_shape=(half, half),
        grid=(pieces,),
        in_specs=[pl.BlockSpec((rows, columns), lambda n: (0, n))] + [whole] * pieces,
        out_specs=(half_spec, half_spec),
        compiler_params=PARAMS,
        cost_estimate=COST,
        name="join",
    )(kept, *arrived)


def finish_kernel(chunks, *refs):
    term_refs, rest = refs[: 3 * chunks], refs[3 * chunks :]
    if len(rest) == 1:
        out_ref = rest[0]
    else:
        before_ref, out_ref, total_ref = rest
    layers, _, width = out_ref.shape
    begin = 0
    for kept_ref, first_ref, second_ref in zip(term_refs[::3], term_refs[1::3], term_refs[2::3]):
        rows = second_ref.shape[0]
        total = kept_ref[...].astype(jnp.float32) + first_ref[...].astype(jnp.float32)
        total = (total + second_ref[...].astype(jnp.float32)).astype(jnp.bfloat16)
        for n in range(layers):
            out_ref[n, begin : begin + rows] = total[:, n * width : (n + 1) * width]
        begin += rows
    if len(rest) == 1:
        return

    @pl.when(pl.program_id(0) == 0)
    def _():
        total_ref[...] = jnp.zeros_like(total_ref)

    total = total_ref[...]
    for n in range(layers):
        total = total + before_ref[n].astype(jnp.float32)
        out_ref[n, begin:] = total.astype(jnp.bfloat16)
    total_ref[...] = total


def finish(layers, *chunks, before=None):
    model = chunks[0][2].shape[1]
    width = model // layers
    group = layers // 2
    operands, in_specs, scratch = [], [], []
    for kept, first, second in chunks:
        operands += [kept, first, second]
        in_specs += [pl.BlockSpec((second.shape[0], group * width), lambda n: (0, n))] * 3
    rows = sum(second.shape[0] for _, _, second in chunks)
    if before is not None:
        more = before.shape[1]
        operands.append(before)
        in_specs.append(pl.BlockSpec((group, more, width), lambda n: (n, 0, 0)))
        scratch.append(pltpu.VMEM((more, width), jnp.float32))
        rows += more
    return pl.pallas_call(
        functools.partial(finish_kernel, len(chunks)),
        out_shape=pltpu.HBM((layers, rows, width), jnp.bfloat16),
        grid=(layers // group,),
        in_specs=in_specs,
        out_specs=pl.BlockSpec((group, rows, width), lambda n: (n, 0, 0)),
        scratch_shapes=scratch,
        compiler_params=PARAMS,
        cost_estimate=COST,
        name="finish",
    )(*operands)


def prefix_kernel(term_ref, out_ref):
    total = term_ref[0].astype(jnp.float32)
    out_ref[0] = term_ref[0]
    for layer in range(1, term_ref.shape[0]):
        total = total + term_ref[layer].astype(jnp.float32)
        out_ref[layer] = total.astype(jnp.bfloat16)


def prefix(terms, rows):
    layers, _, width = terms.shape
    spec = pl.BlockSpec((layers, rows, width), lambda n: (0, 0, 0))
    return pl.pallas_call(
        prefix_kernel,
        out_shape=pltpu.HBM((layers, rows, width), jnp.bfloat16),
        grid=(1,),
        in_specs=[spec],
        out_specs=spec,
        compiler_params=PARAMS,
        cost_estimate=COST,
        name="prefix",
    )(terms)


def norm_kernel(residual_ref, sums_ref, gain_ref, *refs):
    out_ref = refs[-1]
    pieces, rows, width = sums_ref.shape
    square = jnp.zeros((rows, 1), jnp.float32)
    for n in range(pieces):
        stream = residual_ref[:, n * width : (n + 1) * width].astype(jnp.float32)
        stream = stream + sums_ref[n].astype(jnp.float32)
        square = square + jnp.sum(stream * stream, axis=-1, keepdims=True)
    inverse = lax.rsqrt(square / (pieces * width) + 1e-06)
    for n in range(pieces):
        place = slice(n * width, (n + 1) * width)
        stream = residual_ref[:, place].astype(jnp.float32) + sums_ref[n].astype(jnp.float32)
        out_ref[:, place] = (stream * inverse * gain_ref[:, place]).astype(jnp.bfloat16)


def normalize(segments, residual, sums, begin, gain, filled):
    model = residual.shape[1]
    tiles = [
        (first + row) // ROW_TILE for first, count in segments for row in range(0, count, ROW_TILE)
    ]

    def row_tile(n):
        tile = jnp.int32(tiles[0])
        for place, number in enumerate(tiles[1:], 1):
            tile = jnp.where(n == place, number, tile)
        return tile

    row_spec = pl.BlockSpec((ROW_TILE, model), lambda n: (row_tile(n), 0))
    layers, _, width = sums.shape
    in_specs = [
        row_spec,
        pl.BlockSpec((layers, ROW_TILE, width), lambda n: (0, begin // ROW_TILE + n, 0)),
        pl.BlockSpec(gain.shape, lambda n: (0, 0)),
    ]
    operands = [residual, sums, gain]
    aliases = {}
    if filled is not None:
        in_specs.append(pl.BlockSpec(memory_space=pl.ANY))
        operands.append(filled)
        aliases = {3: 0}
    return pl.pallas_call(
        norm_kernel,
        out_shape=jax.ShapeDtypeStruct(residual.shape, jnp.bfloat16),
        grid=(len(tiles),),
        in_specs=in_specs,
        out_specs=row_spec,
        input_output_aliases=aliases,
        compiler_params=PARAMS,
        cost_estimate=COST,
        name="normalize",
    )(*operands)


def add(first, second):
    return (first.astype(jnp.float32) + second.astype(jnp.float32)).astype(jnp.bfloat16)


def after(value, *others):
    return lax.optimization_barrier((value, *others))[0]


def exchange_pairs(chips):
    def near(chip):
        return chip ^ 1

    def far(chip):
        return chips - 1 - chip

    every = [(x, c) for x in range(chips) for c in range(2)]
    cores = [(2 * x + c, 2 * x + 1 - c) for x, c in every]
    first = [(2 * x + c, 2 * (near(x) if c == 0 else far(x)) + c) for x, c in every]
    second = [(2 * x + c, 2 * (far(x) if c == 0 else near(x)) + c) for x, c in every]
    return cores, first, second


def local(
    queries,
    layer_key_rows,
    layer_value_rows,
    vertical_blocks,
    slash_offsets,
    prompt_lengths,
    residual,
    out_weight,
    section_gain,
):
    parts = lax.axis_size("seq")
    layers = lax.axis_size("pipe")
    chips = parts // 2
    tokens, model = queries.shape[1:]
    heads_here = QUERY_HEADS // parts
    place = lax.axis_index("seq")
    vert = lax.dynamic_slice_in_dim(vertical_blocks[0], place * heads_here, heads_here, 0)
    slash = lax.dynamic_slice_in_dim(slash_offsets[0], place * heads_here, heads_here, 0)

    lead = LEAD
    def in_hbm(array):
        return pltpu.with_memory_space_constraint(array, pltpu.HBM)

    queries = in_hbm(queries[0])
    lead_block = pack_lead(parts, lead, queries, in_hbm(layer_key_rows[0]), in_hbm(layer_value_rows[0]))
    rest_block = pack_rest(parts, lead, after(queries, lead_block))
    lead_block = lax.all_to_all(lead_block, "seq", 0, 0)
    rest_block = after(rest_block, lead_block)
    rest_block = lax.all_to_all(rest_block, "seq", 0, 0)

    chip, core = place // 2, place % 2
    near, far = chip ^ 1, chips - 1 - chip
    first_chip = jnp.where(core == 0, near, far)
    second_chip = jnp.where(core == 0, far, near)
    across = chips - 1 - near
    send = jnp.stack([chip, first_chip, second_chip, across]) * 2 + (1 - core)
    keep = jnp.stack([chip, second_chip, first_chip, across]) * 2 + core
    send, keep = send.astype(jnp.int32), keep.astype(jnp.int32)
    to_core, to_first, to_second = exchange_pairs(chips)

    weight = in_hbm(out_weight[0])
    order = jnp.concatenate([send, keep])

    def attend_chunk(segments, *others):
        source = lead_block if segments[0][0] < lead else rest_block
        return attention(
            lead, segments, tokens, after(order, *others), prompt_lengths, vert, slash, source, lead_block
        )

    def project_chunk(context, *others):
        *sent, kept = project(after(context, *others), weight)
        return kept, [lax.ppermute(piece, "seq", to_core) for piece in sent], sent[0]

    def reduce_next(kept, arrived_first, *others):
        rows = kept.shape[0] // 2
        to_send = after(add(kept[rows:], arrived_first[rows:]), *others)
        return lax.ppermute(to_send, "seq", to_second), to_send

    chunk_a, chunk_b, chunk_c = CHUNKS
    context_a = attend_chunk(chunk_a)
    kept_a, pieces_a, token_a = project_chunk(context_a)
    context_b = attend_chunk(chunk_b, token_a)
    kept_a, sent_a = join(after(kept_a, context_b), pieces_a)
    first_a = lax.ppermute(sent_a, "seq", to_first)
    kept_b, pieces_b, token_b = project_chunk(context_b, sent_a)
    context_c = attend_chunk(chunk_c, token_b)
    second_a, next_a = reduce_next(kept_a, first_a, context_c)
    kept_c, pieces_c, token_c = project_chunk(context_c, next_a)
    kept_b, sent_b = join(after(kept_b, token_c, second_a), pieces_b)
    first_b = lax.ppermute(sent_b, "seq", to_first)
    kept_c, sent_c = join(kept_c, pieces_c)
    first_c = lax.ppermute(sent_c, "seq", to_first)
    term_a = finish(layers, (kept_a, first_a, after(second_a, sent_c)))
    terms_a = lax.all_to_all(term_a, "pipe", 0, 0)
    second_b, next_b = reduce_next(kept_b, first_b, term_a)
    prefix_a = prefix(after(terms_a, next_b), terms_a.shape[1])
    sums_a = lax.all_to_all(prefix_a, "pipe", 0, 0)
    second_c, next_c = reduce_next(kept_c, first_c, next_b)
    term_bc = finish(layers, (kept_b, first_b, second_b), (kept_c, first_c, second_c))
    terms_bc = lax.all_to_all(after(term_bc, sums_a), "pipe", 0, 0)
    sums_bc = lax.all_to_all(prefix(terms_bc, terms_bc.shape[1]), "pipe", 0, 0)
    out = normalize(chunk_a, residual, sums_a, 0, section_gain, None)
    out = normalize(chunk_b + chunk_c, residual, sums_bc, 0, section_gain, out)
    return out[None]


def solution(mesh):
    placed = (
        P("pipe", "seq", None),
        P("pipe", "seq", None),
        P("pipe", "seq", None),
        P("pipe", None, None),
        P("pipe", None, None),
        P(),
        P("seq", None),
        P("pipe", "seq", None),
        P("pipe", None),
    )
    return jax.shard_map(
        local, mesh=mesh, in_specs=placed, out_specs=P("pipe", "seq", None), check_vma=False
    )
```

```python
import functools
import math

import jax
import jax.numpy as jnp
from jax import lax
from jax.experimental import pallas as pl
from jax.experimental.pallas import tpu as pltpu
from jax.sharding import PartitionSpec as P

QUERY_HEADS = 64
HEAD_SIZE = 128
BLOCK = 64
LONGEST_PROMPT = 512
CHUNKS = (((0, 48),), ((64, 48),), ((48, 16), (112, 16)))
GROUP = 32
PACK_STEPS = 2
ROW_TILE = 16
LEAD = 48
PIECES = 4
COLUMNS = 1024
AHEAD = 4
FETCHES = 2
NEG = -1e30
COST = pl.CostEstimate(flops=0, transcendentals=0, bytes_accessed=0)
PARAMS = pltpu.CompilerParams(vmem_limit_bytes=16 << 20)


def pack_lead_kernel(q_ref, k_ref, v_ref, out_ref):
    dests, lead_rows, width = out_ref.shape
    rows = lead_rows - GROUP
    for dest in range(dests):
        out_ref[dest, :rows] = q_ref[:, dest * width : (dest + 1) * width]
        column = 0
        for ref in (k_ref, v_ref):
            for begin in range(0, ref.shape[0], GROUP):
                out_ref[dest, rows:, column : column + HEAD_SIZE] = ref[
                    begin : begin + GROUP, dest * HEAD_SIZE : (dest + 1) * HEAD_SIZE
                ]
                column += HEAD_SIZE


def pack_lead(parts, rows, queries, keys, values):
    tokens, model = queries.shape
    width = model // parts
    dests = parts // PACK_STEPS
    return pl.pallas_call(
        pack_lead_kernel,
        out_shape=pltpu.HBM((parts, rows + GROUP, width), jnp.bfloat16),
        grid=(PACK_STEPS,),
        in_specs=[
            pl.BlockSpec((rows, dests * width), lambda n: (0, n)),
            pl.BlockSpec((tokens, dests * HEAD_SIZE), lambda n: (0, n)),
            pl.BlockSpec((tokens, dests * HEAD_SIZE), lambda n: (0, n)),
        ],
        out_specs=pl.BlockSpec((dests, rows + GROUP, width), lambda n: (n, 0, 0)),
        compiler_params=PARAMS,
        cost_estimate=COST,
        name="pack_lead",
    )(queries, keys, values)


def pack_rest_kernel(q_ref, out_ref):
    dests, rows, width = out_ref.shape
    for dest in range(dests):
        out_ref[dest] = q_ref[q_ref.shape[0] - rows :, dest * width : (dest + 1) * width]


def pack_rest(parts, rows, queries):
    tokens, model = queries.shape
    width = model // parts
    dests = parts // PACK_STEPS
    return pl.pallas_call(
        pack_rest_kernel,
        out_shape=pltpu.HBM((parts, tokens - rows, width), jnp.bfloat16),
        grid=(PACK_STEPS,),
        in_specs=[pl.BlockSpec((tokens, dests * width), lambda n: (0, n))],
        out_specs=pl.BlockSpec((dests, tokens - rows, width), lambda n: (n, 0, 0)),
        compiler_params=PARAMS,
        cost_estimate=COST,
        name="pack_rest",
    )(queries)


def attend(queries, key, value, bias):
    heads, rows, _ = bias.shape
    factor = math.log2(math.e) / math.sqrt(HEAD_SIZE)
    scores = lax.dot_general(
        queries, key, (((1,), (1,)), ((), ())), preferred_element_type=jnp.float32
    )
    scores = scores.reshape(bias.shape) + bias
    largest = jnp.max(scores, axis=-1, keepdims=True)
    weights = jnp.exp2((scores - largest) * factor)
    norm = jnp.sum(weights, axis=-1, keepdims=True)
    context = jnp.dot(
        weights.astype(jnp.bfloat16).reshape(heads * rows, -1),
        value,
        preferred_element_type=jnp.float32,
    )
    return (context.reshape(heads, rows, HEAD_SIZE) / norm).astype(jnp.bfloat16)


def gather_keys(kv_ref, kv_scratch, part_rows):
    parts, lead_rows = kv_ref.shape[0], kv_ref.shape[1]
    groups = part_rows // GROUP
    for part in range(parts):
        for group in range(groups):
            begin = part * part_rows + group * GROUP
            for which in range(2):
                column = (which * groups + group) * HEAD_SIZE
                kv_scratch[begin : begin + GROUP, which * HEAD_SIZE : (which + 1) * HEAD_SIZE] = kv_ref[
                    part, lead_rows - GROUP :, column : column + HEAD_SIZE
                ]


def attend_part(
    lead, segments, part, parts, part_rows, lengths_ref, vert_ref, slash_ref, q_ref, kv_scratch, store
):
    heads = vert_ref.shape[0]
    lowest = jnp.int32(0)
    starts = []
    start = 0
    for p in range(lengths_ref.shape[0] - 1):
        start = start + lengths_ref[p]
        starts.append(start)
        lowest = jnp.where(part * part_rows + segments[0][0] >= start, start, lowest)
    shift = int(math.log2(BLOCK))
    rest = lead if segments[0][0] >= lead else 0
    queries = jnp.concatenate(
        [
            q_ref[0, first - rest : first - rest + count, h * HEAD_SIZE : (h + 1) * HEAD_SIZE]
            for h in range(heads)
            for first, count in segments
        ],
        axis=0,
    )
    needed = part + 1 - lax.div(lowest, part_rows)

    def window(count):
        keys = count * part_rows
        begin_part = jnp.clip(part + 1 - count, 0, parts - count)
        begin = pl.multiple_of(begin_part * part_rows, part_rows)
        key_block = lax.shift_right_logical(
            begin + lax.broadcasted_iota(jnp.int32, (heads, keys), 1), shift
        )
        vertical = key_block == vert_ref[:, 0:1]
        for n in range(1, vert_ref.shape[1]):
            vertical = vertical | (key_block == vert_ref[:, n : n + 1])
        biases = []
        for first, count in segments:
            query_first = part * part_rows + first
            query_pos = query_first + lax.broadcasted_iota(jnp.int32, (count, 1), 0)
            own_start = jnp.zeros_like(query_pos)
            for start in starts:
                own_start = jnp.where(query_pos >= start, start, own_start)
            key_pos = begin + lax.broadcasted_iota(jnp.int32, (count, keys), 1)
            token_bias = jnp.where((key_pos <= query_pos) & (key_pos >= own_start), 0.0, NEG)
            offset = lax.shift_right_logical(query_first, shift) - key_block
            hit = vertical
            for n in range(slash_ref.shape[1]):
                hit = hit | (offset == slash_ref[:, n : n + 1])
            head_bias = jnp.where(hit, 0.0, NEG)
            biases.append(token_bias[None] + head_bias[:, None, :])
        key_value = kv_scratch[pl.ds(begin, keys)]
        context = attend(
            queries,
            key_value[:, :HEAD_SIZE],
            key_value[:, HEAD_SIZE:],
            biases[0] if len(biases) == 1 else jnp.concatenate(biases, axis=1),
        )
        for h in range(heads):
            store(h, context[h])

    counts = [2, 3, min(LONGEST_PROMPT // part_rows + 1, parts)]
    for n, count in enumerate(counts):
        fits = needed > counts[n - 1] if n else needed <= count
        if 0 < n < len(counts) - 1:
            fits = fits & (needed <= count)
        pl.when(fits)(functools.partial(window, count))


def context_kernel(
    lead, segments, part_rows, order_ref, lengths_ref, vert_ref, slash_ref, q_ref, kv_ref, out_ref, kv_scratch
):
    step = pl.program_id(0)
    pl.when(step == 0)(lambda: gather_keys(kv_ref, kv_scratch, part_rows))

    def store(head, rows):
        out_ref[0, :, head * HEAD_SIZE : (head + 1) * HEAD_SIZE] = rows

    attend_part(
        lead, segments, order_ref[step], kv_ref.shape[0], part_rows, lengths_ref, vert_ref, slash_ref,
        q_ref, kv_scratch, store,
    )


def attention(lead, segments, part_rows, order, lengths, vert, slash, queries, key_value):
    parts, query_rows = queries.shape[:2]
    blocks = order.shape[0]
    rows = sum(count for _, count in segments)
    width = vert.shape[0] * HEAD_SIZE
    return pl.pallas_call(
        functools.partial(context_kernel, lead, segments, part_rows),
        out_shape=jax.ShapeDtypeStruct((blocks, rows, width), jnp.bfloat16),
        grid_spec=pltpu.PrefetchScalarGridSpec(
            num_scalar_prefetch=2,
            grid=(blocks,),
            in_specs=[
                pl.BlockSpec(vert.shape, lambda n, order, lengths: (0, 0)),
                pl.BlockSpec(slash.shape, lambda n, order, lengths: (0, 0)),
                pl.BlockSpec((1, query_rows, width), lambda n, order, lengths: (order[n], 0, 0)),
                pl.BlockSpec(key_value.shape, lambda n, order, lengths: (0, 0, 0)),
            ],
            out_specs=pl.BlockSpec((1, rows, width), lambda n, order, lengths: (n, 0, 0)),
            scratch_shapes=[pltpu.VMEM((parts * part_rows, 2 * HEAD_SIZE), jnp.bfloat16)],
        ),
        compiler_params=PARAMS,
        cost_estimate=COST,
        name="attention",
    )(order, lengths, vert, slash, queries, key_value)


def project_kernel(context_ref, weight_ref, *refs):
    *send_refs, keep_ref, weight_scratch, sems = refs
    tile = pl.program_id(0)
    tiles = pl.num_programs(0)

    def slot(number):
        return lax.rem(number, weight_scratch.shape[0])

    def fetch(number):
        rows = weight_ref.shape[0] // FETCHES
        return [
            pltpu.make_async_copy(
                weight_ref.at[pl.ds(n * rows, rows), pl.ds(number * COLUMNS, COLUMNS)],
                weight_scratch.at[slot(number), pl.ds(n * rows, rows)],
                sems.at[slot(number), n],
            )
            for n in range(FETCHES)
        ]

    @pl.when(tile == 0)
    def _():
        for number in range(AHEAD):
            for copy in fetch(jnp.int32(number)):
                copy.start()

    @pl.when(tile + AHEAD < tiles)
    def _():
        for copy in fetch(tile + AHEAD):
            copy.start()

    for copy in fetch(tile):
        copy.wait()
    term = jnp.dot(
        context_ref[...].reshape(-1, context_ref.shape[2]),
        weight_scratch[slot(tile)],
        preferred_element_type=jnp.float32,
    ).astype(jnp.bfloat16)
    half = keep_ref.shape[0]
    keep_ref[...] = term[half:]
    per_piece = pl.num_programs(0) // len(send_refs)
    for piece, send_ref in enumerate(send_refs):

        @pl.when((tile >= piece * per_piece) & (tile < (piece + 1) * per_piece))
        def _():
            send_ref[...] = term[:half]


def project(context, weight):
    blocks, block_rows, width = context.shape
    half = blocks * block_rows // 2
    model = weight.shape[1]
    tiles = model // COLUMNS
    per_piece = tiles // PIECES

    def out_spec(piece, count):
        return pl.BlockSpec((half, COLUMNS), lambda n: (0, jnp.clip(n - piece * count, 0, count - 1)))

    return pl.pallas_call(
        project_kernel,
        out_shape=tuple(
            jax.ShapeDtypeStruct((half, model // PIECES), jnp.bfloat16) for _ in range(PIECES)
        )
        + (pltpu.HBM((half, model), jnp.bfloat16),),
        grid=(tiles,),
        in_specs=[
            pl.BlockSpec(context.shape, lambda n: (0, 0, 0)),
            pl.BlockSpec(memory_space=pl.ANY),
        ],
        out_specs=tuple(out_spec(piece, per_piece) for piece in range(PIECES)) + (out_spec(0, tiles),),
        scratch_shapes=[
            pltpu.VMEM((AHEAD + 1, width, COLUMNS), jnp.bfloat16),
            pltpu.SemaphoreType.DMA((AHEAD + 1, FETCHES)),
        ],
        compiler_params=pltpu.CompilerParams(vmem_limit_bytes=24 << 20),
        cost_estimate=COST,
        name="project",
    )(context, weight)


def join_kernel(kept_ref, *refs):
    *arrived_refs, keep_ref, send_ref = refs
    rows = keep_ref.shape[0]
    for piece, arrived_ref in enumerate(arrived_refs):

        @pl.when(pl.program_id(0) == piece)
        def _():
            total = kept_ref[...].astype(jnp.float32) + arrived_ref[...].astype(jnp.float32)
            total = total.astype(jnp.bfloat16)
            keep_ref[...] = total[:rows]
            send_ref[...] = total[rows:]


def join(kept, arrived):
    rows, model = kept.shape
    pieces = len(arrived)
    columns = model // pieces
    half = pltpu.HBM((rows // 2, model), jnp.bfloat16)
    half_spec = pl.BlockSpec((rows // 2, columns), lambda n: (0, n))
    whole = pl.BlockSpec((rows, columns), lambda n: (0, 0))
    return pl.pallas_call(
        join_kernel,
        out_shape=(half, half),
        grid=(pieces,),
        in_specs=[pl.BlockSpec((rows, columns), lambda n: (0, n))] + [whole] * pieces,
        out_specs=(half_spec, half_spec),
        compiler_params=PARAMS,
        cost_estimate=COST,
        name="join",
    )(kept, *arrived)


def finish_kernel(chunks, *refs):
    term_refs, rest = refs[: 3 * chunks], refs[3 * chunks :]
    if len(rest) == 1:
        out_ref = rest[0]
    else:
        before_ref, out_ref, total_ref = rest
    layers, _, width = out_ref.shape
    begin = 0
    for kept_ref, first_ref, second_ref in zip(term_refs[::3], term_refs[1::3], term_refs[2::3]):
        rows = second_ref.shape[0]
        total = kept_ref[...].astype(jnp.float32) + first_ref[...].astype(jnp.float32)
        total = (total + second_ref[...].astype(jnp.float32)).astype(jnp.bfloat16)
        for n in range(layers):
            out_ref[n, begin : begin + rows] = total[:, n * width : (n + 1) * width]
        begin += rows
    if len(rest) == 1:
        return

    @pl.when(pl.program_id(0) == 0)
    def _():
        total_ref[...] = jnp.zeros_like(total_ref)

    total = total_ref[...]
    for n in range(layers):
        total = total + before_ref[n].astype(jnp.float32)
        out_ref[n, begin:] = total.astype(jnp.bfloat16)
    total_ref[...] = total


def finish(layers, *chunks, before=None):
    model = chunks[0][2].shape[1]
    width = model // layers
    group = layers // 2
    operands, in_specs, scratch = [], [], []
    for kept, first, second in chunks:
        operands += [kept, first, second]
        in_specs += [pl.BlockSpec((second.shape[0], group * width), lambda n: (0, n))] * 3
    rows = sum(second.shape[0] for _, _, second in chunks)
    if before is not None:
        more = before.shape[1]
        operands.append(before)
        in_specs.append(pl.BlockSpec((group, more, width), lambda n: (n, 0, 0)))
        scratch.append(pltpu.VMEM((more, width), jnp.float32))
        rows += more
    return pl.pallas_call(
        functools.partial(finish_kernel, len(chunks)),
        out_shape=pltpu.HBM((layers, rows, width), jnp.bfloat16),
        grid=(layers // group,),
        in_specs=in_specs,
        out_specs=pl.BlockSpec((group, rows, width), lambda n: (n, 0, 0)),
        scratch_shapes=scratch,
        compiler_params=PARAMS,
        cost_estimate=COST,
        name="finish",
    )(*operands)


def prefix_kernel(term_ref, out_ref):
    total = term_ref[0].astype(jnp.float32)
    out_ref[0] = term_ref[0]
    for layer in range(1, term_ref.shape[0]):
        total = total + term_ref[layer].astype(jnp.float32)
        out_ref[layer] = total.astype(jnp.bfloat16)


def prefix(terms, rows):
    layers, _, width = terms.shape
    spec = pl.BlockSpec((layers, rows, width), lambda n: (0, 0, 0))
    return pl.pallas_call(
        prefix_kernel,
        out_shape=pltpu.HBM((layers, rows, width), jnp.bfloat16),
        grid=(1,),
        in_specs=[spec],
        out_specs=spec,
        compiler_params=PARAMS,
        cost_estimate=COST,
        name="prefix",
    )(terms)


def norm_kernel(residual_ref, sums_ref, gain_ref, *refs):
    out_ref = refs[-1]
    pieces, rows, width = sums_ref.shape
    square = jnp.zeros((rows, 1), jnp.float32)
    for n in range(pieces):
        stream = residual_ref[:, n * width : (n + 1) * width].astype(jnp.float32)
        stream = stream + sums_ref[n].astype(jnp.float32)
        square = square + jnp.sum(stream * stream, axis=-1, keepdims=True)
    inverse = lax.rsqrt(square / (pieces * width) + 1e-06)
    for n in range(pieces):
        place = slice(n * width, (n + 1) * width)
        stream = residual_ref[:, place].astype(jnp.float32) + sums_ref[n].astype(jnp.float32)
        out_ref[:, place] = (stream * inverse * gain_ref[:, place]).astype(jnp.bfloat16)


def normalize(segments, residual, sums, begin, gain, filled):
    model = residual.shape[1]
    tiles = [
        (first + row) // ROW_TILE for first, count in segments for row in range(0, count, ROW_TILE)
    ]

    def row_tile(n):
        tile = jnp.int32(tiles[0])
        for place, number in enumerate(tiles[1:], 1):
            tile = jnp.where(n == place, number, tile)
        return tile

    row_spec = pl.BlockSpec((ROW_TILE, model), lambda n: (row_tile(n), 0))
    layers, _, width = sums.shape
    in_specs = [
        row_spec,
        pl.BlockSpec((layers, ROW_TILE, width), lambda n: (0, begin // ROW_TILE + n, 0)),
        pl.BlockSpec(gain.shape, lambda n: (0, 0)),
    ]
    operands = [residual, sums, gain]
    aliases = {}
    if filled is not None:
        in_specs.append(pl.BlockSpec(memory_space=pl.ANY))
        operands.append(filled)
        aliases = {3: 0}
    return pl.pallas_call(
        norm_kernel,
        out_shape=jax.ShapeDtypeStruct(residual.shape, jnp.bfloat16),
        grid=(len(tiles),),
        in_specs=in_specs,
        out_specs=row_spec,
        input_output_aliases=aliases,
        compiler_params=PARAMS,
        cost_estimate=COST,
        name="normalize",
    )(*operands)


def add(first, second):
    return (first.astype(jnp.float32) + second.astype(jnp.float32)).astype(jnp.bfloat16)


def after(value, *others):
    return lax.optimization_barrier((value, *others))[0]


def exchange_pairs(chips):
    def near(chip):
        return chip ^ 1

    def far(chip):
        return chips - 1 - chip

    every = [(x, c) for x in range(chips) for c in range(2)]
    cores = [(2 * x + c, 2 * x + 1 - c) for x, c in every]
    first = [(2 * x + c, 2 * (near(x) if c == 0 else far(x)) + c) for x, c in every]
    second = [(2 * x + c, 2 * (far(x) if c == 0 else near(x)) + c) for x, c in every]
    return cores, first, second


def local(
    queries,
    layer_key_rows,
    layer_value_rows,
    vertical_blocks,
    slash_offsets,
    prompt_lengths,
    residual,
    out_weight,
    section_gain,
):
    parts = lax.axis_size("seq")
    layers = lax.axis_size("pipe")
    chips = parts // 2
    tokens, model = queries.shape[1:]
    heads_here = QUERY_HEADS // parts
    place = lax.axis_index("seq")
    vert = lax.dynamic_slice_in_dim(vertical_blocks[0], place * heads_here, heads_here, 0)
    slash = lax.dynamic_slice_in_dim(slash_offsets[0], place * heads_here, heads_here, 0)

    lead = LEAD
    def in_hbm(array):
        return pltpu.with_memory_space_constraint(array, pltpu.HBM)

    queries = in_hbm(queries[0])
    lead_block = pack_lead(parts, lead, queries, in_hbm(layer_key_rows[0]), in_hbm(layer_value_rows[0]))
    rest_block = pack_rest(parts, lead, after(queries, lead_block))
    lead_block = lax.all_to_all(lead_block, "seq", 0, 0)
    rest_block = after(rest_block, lead_block)
    rest_block = lax.all_to_all(rest_block, "seq", 0, 0)

    chip, core = place // 2, place % 2
    near, far = chip ^ 1, chips - 1 - chip
    first_chip = jnp.where(core == 0, near, far)
    second_chip = jnp.where(core == 0, far, near)
    across = chips - 1 - near
    send = jnp.stack([chip, first_chip, second_chip, across]) * 2 + (1 - core)
    keep = jnp.stack([chip, second_chip, first_chip, across]) * 2 + core
    send, keep = send.astype(jnp.int32), keep.astype(jnp.int32)
    to_core, to_first, to_second = exchange_pairs(chips)

    weight = in_hbm(out_weight[0])
    order = jnp.concatenate([send, keep])

    def attend_chunk(segments, *others):
        source = lead_block if segments[0][0] < lead else rest_block
        return attention(
            lead, segments, tokens, after(order, *others), prompt_lengths, vert, slash, source, lead_block
        )

    def project_chunk(context, *others):
        *sent, kept = project(after(context, *others), weight)
        return kept, [lax.ppermute(piece, "seq", to_core) for piece in sent], sent[0]

    def reduce_next(kept, arrived_first, *others):
        rows = kept.shape[0] // 2
        to_send = after(add(kept[rows:], arrived_first[rows:]), *others)
        return lax.ppermute(to_send, "seq", to_second), to_send

    chunk_a, chunk_b, chunk_c = CHUNKS
    context_a = attend_chunk(chunk_a)
    kept_a, pieces_a, token_a = project_chunk(context_a)
    context_b = attend_chunk(chunk_b, token_a)
    kept_a, sent_a = join(after(kept_a, context_b), pieces_a)
    first_a = lax.ppermute(sent_a, "seq", to_first)
    kept_b, pieces_b, token_b = project_chunk(context_b, sent_a)
    context_c = attend_chunk(chunk_c, token_b)
    second_a, next_a = reduce_next(kept_a, first_a, context_c)
    kept_c, pieces_c, token_c = project_chunk(context_c, next_a)
    kept_b, sent_b = join(after(kept_b, token_c, second_a), pieces_b)
    first_b = lax.ppermute(sent_b, "seq", to_first)
    term_a = finish(layers, (kept_a, first_a, after(second_a, sent_b)))
    terms_a = lax.all_to_all(term_a, "pipe", 0, 0)
    kept_c, sent_c = join(after(kept_c, term_a), pieces_c)
    first_c = lax.ppermute(sent_c, "seq", to_first)
    second_b, next_b = reduce_next(kept_b, first_b, sent_c)
    prefix_a = prefix(after(terms_a, next_b), terms_a.shape[1])
    sums_a = lax.all_to_all(prefix_a, "pipe", 0, 0)
    second_c, next_c = reduce_next(kept_c, first_c, next_b)
    term_bc = finish(layers, (kept_b, first_b, second_b), (kept_c, first_c, second_c))
    terms_bc = lax.all_to_all(after(term_bc, sums_a), "pipe", 0, 0)
    sums_bc = lax.all_to_all(prefix(terms_bc, terms_bc.shape[1]), "pipe", 0, 0)
    out = normalize(chunk_a, residual, sums_a, 0, section_gain, None)
    out = normalize(chunk_b + chunk_c, residual, sums_bc, 0, section_gain, out)
    return out[None]


def solution(mesh):
    placed = (
        P("pipe", "seq", None),
        P("pipe", "seq", None),
        P("pipe", "seq", None),
        P("pipe", None, None),
        P("pipe", None, None),
        P(),
        P("seq", None),
        P("pipe", "seq", None),
        P("pipe", None),
    )
    return jax.shard_map(
        local, mesh=mesh, in_specs=placed, out_specs=P("pipe", "seq", None), check_vma=False
    )
```

```python
import functools
import math

import jax
import jax.numpy as jnp
from jax import lax
from jax.experimental import pallas as pl
from jax.experimental.pallas import tpu as pltpu
from jax.sharding import PartitionSpec as P

QUERY_HEADS = 64
HEAD_SIZE = 128
BLOCK = 64
LONGEST_PROMPT = 512
CHUNKS = (((0, 48),), ((64, 48),), ((48, 16), (112, 16)))
GROUP = 32
PACK_STEPS = 2
ROW_TILE = 16
LEAD = 48
PIECES = 4
COLUMNS = 1024
AHEAD = 4
FETCHES = 2
JOIN_TILES = 2
NEG = -1e30
COST = pl.CostEstimate(flops=0, transcendentals=0, bytes_accessed=0)
PARAMS = pltpu.CompilerParams(vmem_limit_bytes=16 << 20)


def pack_lead_kernel(q_ref, k_ref, v_ref, out_ref):
    dests, lead_rows, width = out_ref.shape
    rows = lead_rows - GROUP
    for dest in range(dests):
        out_ref[dest, :rows] = q_ref[:, dest * width : (dest + 1) * width]
        column = 0
        for ref in (k_ref, v_ref):
            for begin in range(0, ref.shape[0], GROUP):
                out_ref[dest, rows:, column : column + HEAD_SIZE] = ref[
                    begin : begin + GROUP, dest * HEAD_SIZE : (dest + 1) * HEAD_SIZE
                ]
                column += HEAD_SIZE


def pack_lead(parts, rows, queries, keys, values):
    tokens, model = queries.shape
    width = model // parts
    dests = parts // PACK_STEPS
    return pl.pallas_call(
        pack_lead_kernel,
        out_shape=pltpu.HBM((parts, rows + GROUP, width), jnp.bfloat16),
        grid=(PACK_STEPS,),
        in_specs=[
            pl.BlockSpec((rows, dests * width), lambda n: (0, n)),
            pl.BlockSpec((tokens, dests * HEAD_SIZE), lambda n: (0, n)),
            pl.BlockSpec((tokens, dests * HEAD_SIZE), lambda n: (0, n)),
        ],
        out_specs=pl.BlockSpec((dests, rows + GROUP, width), lambda n: (n, 0, 0)),
        compiler_params=PARAMS,
        cost_estimate=COST,
        name="pack_lead",
    )(queries, keys, values)


def pack_rest_kernel(q_ref, out_ref):
    dests, rows, width = out_ref.shape
    for dest in range(dests):
        out_ref[dest] = q_ref[q_ref.shape[0] - rows :, dest * width : (dest + 1) * width]


def pack_rest(parts, rows, queries):
    tokens, model = queries.shape
    width = model // parts
    dests = parts // PACK_STEPS
    return pl.pallas_call(
        pack_rest_kernel,
        out_shape=pltpu.HBM((parts, tokens - rows, width), jnp.bfloat16),
        grid=(PACK_STEPS,),
        in_specs=[pl.BlockSpec((tokens, dests * width), lambda n: (0, n))],
        out_specs=pl.BlockSpec((dests, tokens - rows, width), lambda n: (n, 0, 0)),
        compiler_params=PARAMS,
        cost_estimate=COST,
        name="pack_rest",
    )(queries)


def attend(queries, key, value, bias):
    heads, rows, _ = bias.shape
    factor = math.log2(math.e) / math.sqrt(HEAD_SIZE)
    scores = lax.dot_general(
        queries, key, (((1,), (1,)), ((), ())), preferred_element_type=jnp.float32
    )
    scores = scores.reshape(bias.shape) + bias
    largest = jnp.max(scores, axis=-1, keepdims=True)
    weights = jnp.exp2((scores - largest) * factor)
    norm = jnp.sum(weights, axis=-1, keepdims=True)
    context = jnp.dot(
        weights.astype(jnp.bfloat16).reshape(heads * rows, -1),
        value,
        preferred_element_type=jnp.float32,
    )
    return (context.reshape(heads, rows, HEAD_SIZE) / norm).astype(jnp.bfloat16)


def gather_keys(kv_ref, kv_scratch, part_rows):
    parts, lead_rows = kv_ref.shape[0], kv_ref.shape[1]
    groups = part_rows // GROUP
    for part in range(parts):
        for group in range(groups):
            begin = part * part_rows + group * GROUP
            for which in range(2):
                column = (which * groups + group) * HEAD_SIZE
                kv_scratch[begin : begin + GROUP, which * HEAD_SIZE : (which + 1) * HEAD_SIZE] = kv_ref[
                    part, lead_rows - GROUP :, column : column + HEAD_SIZE
                ]


def attend_part(
    lead, segments, part, parts, part_rows, lengths_ref, vert_ref, slash_ref, q_ref, kv_scratch, store
):
    heads = vert_ref.shape[0]
    lowest = jnp.int32(0)
    starts = []
    start = 0
    for p in range(lengths_ref.shape[0] - 1):
        start = start + lengths_ref[p]
        starts.append(start)
        lowest = jnp.where(part * part_rows + segments[0][0] >= start, start, lowest)
    shift = int(math.log2(BLOCK))
    rest = lead if segments[0][0] >= lead else 0
    queries = jnp.concatenate(
        [
            q_ref[0, first - rest : first - rest + count, h * HEAD_SIZE : (h + 1) * HEAD_SIZE]
            for h in range(heads)
            for first, count in segments
        ],
        axis=0,
    )
    needed = part + 1 - lax.div(lowest, part_rows)

    def window(count):
        keys = count * part_rows
        begin_part = jnp.clip(part + 1 - count, 0, parts - count)
        begin = pl.multiple_of(begin_part * part_rows, part_rows)
        key_block = lax.shift_right_logical(
            begin + lax.broadcasted_iota(jnp.int32, (heads, keys), 1), shift
        )
        vertical = key_block == vert_ref[:, 0:1]
        for n in range(1, vert_ref.shape[1]):
            vertical = vertical | (key_block == vert_ref[:, n : n + 1])
        biases = []
        for first, count in segments:
            query_first = part * part_rows + first
            query_pos = query_first + lax.broadcasted_iota(jnp.int32, (count, 1), 0)
            own_start = jnp.zeros_like(query_pos)
            for start in starts:
                own_start = jnp.where(query_pos >= start, start, own_start)
            key_pos = begin + lax.broadcasted_iota(jnp.int32, (count, keys), 1)
            token_bias = jnp.where((key_pos <= query_pos) & (key_pos >= own_start), 0.0, NEG)
            offset = lax.shift_right_logical(query_first, shift) - key_block
            hit = vertical
            for n in range(slash_ref.shape[1]):
                hit = hit | (offset == slash_ref[:, n : n + 1])
            head_bias = jnp.where(hit, 0.0, NEG)
            biases.append(token_bias[None] + head_bias[:, None, :])
        key_value = kv_scratch[pl.ds(begin, keys)]
        context = attend(
            queries,
            key_value[:, :HEAD_SIZE],
            key_value[:, HEAD_SIZE:],
            biases[0] if len(biases) == 1 else jnp.concatenate(biases, axis=1),
        )
        for h in range(heads):
            store(h, context[h])

    counts = [2, 3, min(LONGEST_PROMPT // part_rows + 1, parts)]
    for n, count in enumerate(counts):
        fits = needed > counts[n - 1] if n else needed <= count
        if 0 < n < len(counts) - 1:
            fits = fits & (needed <= count)
        pl.when(fits)(functools.partial(window, count))


def context_kernel(
    lead, segments, part_rows, order_ref, lengths_ref, vert_ref, slash_ref, q_ref, kv_ref, out_ref, kv_scratch
):
    step = pl.program_id(0)
    pl.when(step == 0)(lambda: gather_keys(kv_ref, kv_scratch, part_rows))

    def store(head, rows):
        out_ref[0, :, head * HEAD_SIZE : (head + 1) * HEAD_SIZE] = rows

    attend_part(
        lead, segments, order_ref[step], kv_ref.shape[0], part_rows, lengths_ref, vert_ref, slash_ref,
        q_ref, kv_scratch, store,
    )


def attention(lead, segments, part_rows, order, lengths, vert, slash, queries, key_value):
    parts, query_rows = queries.shape[:2]
    blocks = order.shape[0]
    rows = sum(count for _, count in segments)
    width = vert.shape[0] * HEAD_SIZE
    return pl.pallas_call(
        functools.partial(context_kernel, lead, segments, part_rows),
        out_shape=jax.ShapeDtypeStruct((blocks, rows, width), jnp.bfloat16),
        grid_spec=pltpu.PrefetchScalarGridSpec(
            num_scalar_prefetch=2,
            grid=(blocks,),
            in_specs=[
                pl.BlockSpec(vert.shape, lambda n, order, lengths: (0, 0)),
                pl.BlockSpec(slash.shape, lambda n, order, lengths: (0, 0)),
                pl.BlockSpec((1, query_rows, width), lambda n, order, lengths: (order[n], 0, 0)),
                pl.BlockSpec(key_value.shape, lambda n, order, lengths: (0, 0, 0)),
            ],
            out_specs=pl.BlockSpec((1, rows, width), lambda n, order, lengths: (n, 0, 0)),
            scratch_shapes=[pltpu.VMEM((parts * part_rows, 2 * HEAD_SIZE), jnp.bfloat16)],
        ),
        compiler_params=PARAMS,
        cost_estimate=COST,
        name="attention",
    )(order, lengths, vert, slash, queries, key_value)


def project_kernel(context_ref, weight_ref, *refs):
    *send_refs, keep_ref, weight_scratch, sems = refs
    tile = pl.program_id(0)
    tiles = pl.num_programs(0)

    def slot(number):
        return lax.rem(number, weight_scratch.shape[0])

    def fetch(number):
        rows = weight_ref.shape[0] // FETCHES
        return [
            pltpu.make_async_copy(
                weight_ref.at[pl.ds(n * rows, rows), pl.ds(number * COLUMNS, COLUMNS)],
                weight_scratch.at[slot(number), pl.ds(n * rows, rows)],
                sems.at[slot(number), n],
            )
            for n in range(FETCHES)
        ]

    @pl.when(tile == 0)
    def _():
        for number in range(AHEAD):
            for copy in fetch(jnp.int32(number)):
                copy.start()

    @pl.when(tile + AHEAD < tiles)
    def _():
        for copy in fetch(tile + AHEAD):
            copy.start()

    for copy in fetch(tile):
        copy.wait()
    term = jnp.dot(
        context_ref[...].reshape(-1, context_ref.shape[2]),
        weight_scratch[slot(tile)],
        preferred_element_type=jnp.float32,
    ).astype(jnp.bfloat16)
    half = keep_ref.shape[0]
    keep_ref[...] = term[half:]
    per_piece = pl.num_programs(0) // len(send_refs)
    for piece, send_ref in enumerate(send_refs):

        @pl.when((tile >= piece * per_piece) & (tile < (piece + 1) * per_piece))
        def _():
            send_ref[...] = term[:half]


def project(context, weight):
    blocks, block_rows, width = context.shape
    half = blocks * block_rows // 2
    model = weight.shape[1]
    tiles = model // COLUMNS
    per_piece = tiles // PIECES

    def out_spec(piece, count):
        return pl.BlockSpec((half, COLUMNS), lambda n: (0, jnp.clip(n - piece * count, 0, count - 1)))

    return pl.pallas_call(
        project_kernel,
        out_shape=tuple(
            jax.ShapeDtypeStruct((half, model // PIECES), jnp.bfloat16) for _ in range(PIECES)
        )
        + (pltpu.HBM((half, model), jnp.bfloat16),),
        grid=(tiles,),
        in_specs=[
            pl.BlockSpec(context.shape, lambda n: (0, 0, 0)),
            pl.BlockSpec(memory_space=pl.ANY),
        ],
        out_specs=tuple(out_spec(piece, per_piece) for piece in range(PIECES)) + (out_spec(0, tiles),),
        scratch_shapes=[
            pltpu.VMEM((AHEAD + 1, width, COLUMNS), jnp.bfloat16),
            pltpu.SemaphoreType.DMA((AHEAD + 1, FETCHES)),
        ],
        compiler_params=pltpu.CompilerParams(vmem_limit_bytes=24 << 20),
        cost_estimate=COST,
        name="project",
    )(context, weight)


def join_kernel(kept_ref, *refs):
    *arrived_refs, keep_ref, send_ref = refs
    rows = keep_ref.shape[0]
    for piece, arrived_ref in enumerate(arrived_refs):

        @pl.when(lax.div(pl.program_id(0), JOIN_TILES) == piece)
        def _():
            total = kept_ref[...].astype(jnp.float32) + arrived_ref[...].astype(jnp.float32)
            total = total.astype(jnp.bfloat16)
            keep_ref[...] = total[:rows]
            send_ref[...] = total[rows:]


def join(kept, arrived):
    rows, model = kept.shape
    pieces = len(arrived)
    columns = model // pieces // JOIN_TILES
    half = pltpu.HBM((rows // 2, model), jnp.bfloat16)
    half_spec = pl.BlockSpec((rows // 2, columns), lambda n: (0, n))

    def piece_spec(piece):
        return pl.BlockSpec(
            (rows, columns), lambda n: (0, jnp.clip(n - piece * JOIN_TILES, 0, JOIN_TILES - 1))
        )

    return pl.pallas_call(
        join_kernel,
        out_shape=(half, half),
        grid=(pieces * JOIN_TILES,),
        in_specs=[pl.BlockSpec((rows, columns), lambda n: (0, n))]
        + [piece_spec(piece) for piece in range(pieces)],
        out_specs=(half_spec, half_spec),
        compiler_params=PARAMS,
        cost_estimate=COST,
        name="join",
    )(kept, *arrived)


def finish_kernel(chunks, *refs):
    term_refs, rest = refs[: 3 * chunks], refs[3 * chunks :]
    if len(rest) == 1:
        out_ref = rest[0]
    else:
        before_ref, out_ref, total_ref = rest
    layers, _, width = out_ref.shape
    begin = 0
    for kept_ref, first_ref, second_ref in zip(term_refs[::3], term_refs[1::3], term_refs[2::3]):
        rows = second_ref.shape[0]
        total = kept_ref[...].astype(jnp.float32) + first_ref[...].astype(jnp.float32)
        total = (total + second_ref[...].astype(jnp.float32)).astype(jnp.bfloat16)
        for n in range(layers):
            out_ref[n, begin : begin + rows] = total[:, n * width : (n + 1) * width]
        begin += rows
    if len(rest) == 1:
        return

    @pl.when(pl.program_id(0) == 0)
    def _():
        total_ref[...] = jnp.zeros_like(total_ref)

    total = total_ref[...]
    for n in range(layers):
        total = total + before_ref[n].astype(jnp.float32)
        out_ref[n, begin:] = total.astype(jnp.bfloat16)
    total_ref[...] = total


def finish(layers, *chunks, before=None):
    model = chunks[0][2].shape[1]
    width = model // layers
    group = layers // 2
    operands, in_specs, scratch = [], [], []
    for kept, first, second in chunks:
        operands += [kept, first, second]
        in_specs += [pl.BlockSpec((second.shape[0], group * width), lambda n: (0, n))] * 3
    rows = sum(second.shape[0] for _, _, second in chunks)
    if before is not None:
        more = before.shape[1]
        operands.append(before)
        in_specs.append(pl.BlockSpec((group, more, width), lambda n: (n, 0, 0)))
        scratch.append(pltpu.VMEM((more, width), jnp.float32))
        rows += more
    return pl.pallas_call(
        functools.partial(finish_kernel, len(chunks)),
        out_shape=pltpu.HBM((layers, rows, width), jnp.bfloat16),
        grid=(layers // group,),
        in_specs=in_specs,
        out_specs=pl.BlockSpec((group, rows, width), lambda n: (n, 0, 0)),
        scratch_shapes=scratch,
        compiler_params=PARAMS,
        cost_estimate=COST,
        name="finish",
    )(*operands)


def prefix_kernel(term_ref, out_ref):
    total = term_ref[0].astype(jnp.float32)
    out_ref[0] = term_ref[0]
    for layer in range(1, term_ref.shape[0]):
        total = total + term_ref[layer].astype(jnp.float32)
        out_ref[layer] = total.astype(jnp.bfloat16)


def prefix(terms, rows):
    layers, _, width = terms.shape
    spec = pl.BlockSpec((layers, rows, width), lambda n: (0, 0, 0))
    return pl.pallas_call(
        prefix_kernel,
        out_shape=pltpu.HBM((layers, rows, width), jnp.bfloat16),
        grid=(1,),
        in_specs=[spec],
        out_specs=spec,
        compiler_params=PARAMS,
        cost_estimate=COST,
        name="prefix",
    )(terms)


def norm_kernel(residual_ref, sums_ref, gain_ref, *refs):
    out_ref = refs[-1]
    pieces, rows, width = sums_ref.shape
    square = jnp.zeros((rows, 1), jnp.float32)
    for n in range(pieces):
        stream = residual_ref[:, n * width : (n + 1) * width].astype(jnp.float32)
        stream = stream + sums_ref[n].astype(jnp.float32)
        square = square + jnp.sum(stream * stream, axis=-1, keepdims=True)
    inverse = lax.rsqrt(square / (pieces * width) + 1e-06)
    for n in range(pieces):
        place = slice(n * width, (n + 1) * width)
        stream = residual_ref[:, place].astype(jnp.float32) + sums_ref[n].astype(jnp.float32)
        out_ref[:, place] = (stream * inverse * gain_ref[:, place]).astype(jnp.bfloat16)


def normalize(segments, residual, sums, begin, gain, filled):
    model = residual.shape[1]
    tiles = [
        (first + row) // ROW_TILE for first, count in segments for row in range(0, count, ROW_TILE)
    ]

    def row_tile(n):
        tile = jnp.int32(tiles[0])
        for place, number in enumerate(tiles[1:], 1):
            tile = jnp.where(n == place, number, tile)
        return tile

    row_spec = pl.BlockSpec((ROW_TILE, model), lambda n: (row_tile(n), 0))
    layers, _, width = sums.shape
    in_specs = [
        row_spec,
        pl.BlockSpec((layers, ROW_TILE, width), lambda n: (0, begin // ROW_TILE + n, 0)),
        pl.BlockSpec(gain.shape, lambda n: (0, 0)),
    ]
    operands = [residual, sums, gain]
    aliases = {}
    if filled is not None:
        in_specs.append(pl.BlockSpec(memory_space=pl.ANY))
        operands.append(filled)
        aliases = {3: 0}
    return pl.pallas_call(
        norm_kernel,
        out_shape=jax.ShapeDtypeStruct(residual.shape, jnp.bfloat16),
        grid=(len(tiles),),
        in_specs=in_specs,
        out_specs=row_spec,
        input_output_aliases=aliases,
        compiler_params=PARAMS,
        cost_estimate=COST,
        name="normalize",
    )(*operands)


def add(first, second):
    return (first.astype(jnp.float32) + second.astype(jnp.float32)).astype(jnp.bfloat16)


def after(value, *others):
    return lax.optimization_barrier((value, *others))[0]


def exchange_pairs(chips):
    def near(chip):
        return chip ^ 1

    def far(chip):
        return chips - 1 - chip

    every = [(x, c) for x in range(chips) for c in range(2)]
    cores = [(2 * x + c, 2 * x + 1 - c) for x, c in every]
    first = [(2 * x + c, 2 * (near(x) if c == 0 else far(x)) + c) for x, c in every]
    second = [(2 * x + c, 2 * (far(x) if c == 0 else near(x)) + c) for x, c in every]
    return cores, first, second


def local(
    queries,
    layer_key_rows,
    layer_value_rows,
    vertical_blocks,
    slash_offsets,
    prompt_lengths,
    residual,
    out_weight,
    section_gain,
):
    parts = lax.axis_size("seq")
    layers = lax.axis_size("pipe")
    chips = parts // 2
    tokens, model = queries.shape[1:]
    heads_here = QUERY_HEADS // parts
    place = lax.axis_index("seq")
    vert = lax.dynamic_slice_in_dim(vertical_blocks[0], place * heads_here, heads_here, 0)
    slash = lax.dynamic_slice_in_dim(slash_offsets[0], place * heads_here, heads_here, 0)

    lead = LEAD
    def in_hbm(array):
        return pltpu.with_memory_space_constraint(array, pltpu.HBM)

    queries = in_hbm(queries[0])
    lead_block = pack_lead(parts, lead, queries, in_hbm(layer_key_rows[0]), in_hbm(layer_value_rows[0]))
    rest_block = pack_rest(parts, lead, after(queries, lead_block))
    lead_block = lax.all_to_all(lead_block, "seq", 0, 0)
    rest_block = after(rest_block, lead_block)
    rest_block = lax.all_to_all(rest_block, "seq", 0, 0)

    chip, core = place // 2, place % 2
    near, far = chip ^ 1, chips - 1 - chip
    first_chip = jnp.where(core == 0, near, far)
    second_chip = jnp.where(core == 0, far, near)
    across = chips - 1 - near
    send = jnp.stack([chip, first_chip, second_chip, across]) * 2 + (1 - core)
    keep = jnp.stack([chip, second_chip, first_chip, across]) * 2 + core
    send, keep = send.astype(jnp.int32), keep.astype(jnp.int32)
    to_core, to_first, to_second = exchange_pairs(chips)

    weight = in_hbm(out_weight[0])
    order = jnp.concatenate([send, keep])

    def attend_chunk(segments, *others):
        source = lead_block if segments[0][0] < lead else rest_block
        return attention(
            lead, segments, tokens, after(order, *others), prompt_lengths, vert, slash, source, lead_block
        )

    def project_chunk(context, *others):
        *sent, kept = project(after(context, *others), weight)
        return kept, [lax.ppermute(piece, "seq", to_core) for piece in sent], sent[0]

    def reduce_next(kept, arrived_first, *others):
        rows = kept.shape[0] // 2
        to_send = after(add(kept[rows:], arrived_first[rows:]), *others)
        return lax.ppermute(to_send, "seq", to_second), to_send

    chunk_a, chunk_b, chunk_c = CHUNKS
    context_a = attend_chunk(chunk_a)
    kept_a, pieces_a, token_a = project_chunk(context_a)
    context_b = attend_chunk(chunk_b, token_a)
    kept_a, sent_a = join(after(kept_a, context_b), pieces_a)
    first_a = lax.ppermute(sent_a, "seq", to_first)
    kept_b, pieces_b, token_b = project_chunk(context_b, sent_a)
    context_c = attend_chunk(chunk_c, token_b)
    second_a, next_a = reduce_next(kept_a, first_a, context_c)
    kept_c, pieces_c, token_c = project_chunk(context_c, next_a)
    kept_b, sent_b = join(after(kept_b, token_c, second_a), pieces_b)
    first_b = lax.ppermute(sent_b, "seq", to_first)
    term_a = finish(layers, (kept_a, first_a, after(second_a, sent_b)))
    terms_a = lax.all_to_all(term_a, "pipe", 0, 0)
    kept_c, sent_c = join(after(kept_c, term_a), pieces_c)
    first_c = lax.ppermute(sent_c, "seq", to_first)
    second_b, next_b = reduce_next(kept_b, first_b, sent_c)
    prefix_a = prefix(after(terms_a, next_b), terms_a.shape[1])
    sums_a = lax.all_to_all(prefix_a, "pipe", 0, 0)
    second_c, next_c = reduce_next(kept_c, first_c, next_b)
    term_bc = finish(layers, (kept_b, first_b, second_b), (kept_c, first_c, second_c))
    terms_bc = lax.all_to_all(after(term_bc, sums_a), "pipe", 0, 0)
    sums_bc = lax.all_to_all(prefix(terms_bc, terms_bc.shape[1]), "pipe", 0, 0)
    out = normalize(chunk_a, residual, sums_a, 0, section_gain, None)
    out = normalize(chunk_b + chunk_c, residual, sums_bc, 0, section_gain, out)
    return out[None]


def solution(mesh):
    placed = (
        P("pipe", "seq", None),
        P("pipe", "seq", None),
        P("pipe", "seq", None),
        P("pipe", None, None),
        P("pipe", None, None),
        P(),
        P("seq", None),
        P("pipe", "seq", None),
        P("pipe", None),
    )
    return jax.shard_map(
        local, mesh=mesh, in_specs=placed, out_specs=P("pipe", "seq", None), check_vma=False
    )
```
